32 devices in a mesh: chan: 2 (over x), bl: 16 (over z, y, core).
Axes of the slice: x: 2, y: 2, z: 4, core: 2. Of those that a mesh axis runs over, the one named last changes fastest.
Arguments:
- vis: bfloat16 [2, 8, 8192, 256], P(None, 'chan', 'bl'), may hold values from -6 to 6
- station_pair_index: int32 [8192, 2], P('bl'), may hold values from 0 to 511
- station_coords: float32 [512, 2], replicated, may hold values from -1 to 1
- dir_lm: float32 [60, 2], replicated, may hold values from -0.5 to 0.5
- time_beam: float32 [60, 256], replicated, may hold values from -6 to 6
- dir_cluster: int32 [60], replicated, may hold values from 0 to 11, as said below
- seed_block: int32 [64, 256, 8], P('bl'), may hold values from -8 to 8
Outputs:
- clean: bfloat16 [2, 8, 8192, 256], P(None, 'chan', 'bl')
- gains: float32 [64, 12], P('bl')
- consensus: float32 [12], replicated
The draws below stay inside these ranges and needn't reach their ends.
Inputs may be any that keep to these rules, and one draw needn't show every extreme that they name: `dir_cluster`: every cluster is named by some direction.
All inputs are finite; a program needn't handle non-finite values.
Results may differ from the reference program's by a relative error of at most 0.0029.
The reference program's roundings to bfloat16 on the way (of `response` and `basis`) count: a program that leaves them out, or rounds other values in their place, can miss the bound.
Values sent between devices are 32-bit elements; how exact they have to be, the bound alone decides.
A program may use at most 64 MiB of HBM per device.

```python
import jax
import jax.numpy as jnp
from jax import lax

TIME_SAMPLES = 256
DIRS = 60
STATION_COUNT = 512
RANK = 8
CL = 12
TILE = 128
SUB_ITERS = 3
ADMM_ITERS = 6
CHANNEL_COUNT = 8
BASELINE_COUNT = 8192
TILES = 64


def draw_dir_cluster(key, part):
    first_key, second_key, third_key = jax.random.split(key, 3)
    base = jax.random.permutation(first_key, CL).astype(jnp.int32)
    others = jax.random.randint(second_key, (DIRS - CL,), 0, CL).astype(jnp.int32)
    joined = jnp.concatenate([base, others])
    return jax.random.permutation(third_key, joined).astype(jnp.int32)


def set_ends(values, stream_key, low, high):
    place = [jax.random.randint(jax.random.fold_in(stream_key, axis), (), 0, length) for axis, length in enumerate(values.shape)]
    longest = values.shape.index(max(values.shape))
    next_to = place[:longest] + [(place[longest] + 1) % values.shape[longest]] + place[longest + 1:]
    return values.at[tuple(place)].set(low).at[tuple(next_to)].set(high)


def shard_levels(key, extent, shards, low, high):
    level = 1.0
    for position, blocks in shards:
        draws = jax.random.uniform(jax.random.fold_in(jax.random.fold_in(key, 6), position), (blocks,), jnp.float32, low / len(shards), high / len(shards))
        level = level * jnp.repeat(jnp.exp(draws), extent[position] // blocks).reshape((-1,) + (1,) * (len(extent) - 1 - position))
    return level


def noise(own_key, shape, scale, reach, pieces=(), kind=jnp.bfloat16):
    array = scale * jax.random.normal(own_key, shape, jnp.float32)
    if pieces:
        array = array * shard_levels(own_key, shape, pieces, -0.22, 0.18)
    return jnp.clip(array, -reach, reach).astype(kind)


def setup_inputs(seed: int = 0) -> dict:
    splits = jax.random.split(jax.random.key(seed), 8)
    vis = noise(splits[0], (2, CHANNEL_COUNT, BASELINE_COUNT, TIME_SAMPLES), 1.0, 6.0, ((1, 2), (2, 16)))
    station_pair_index = set_ends(jax.random.randint(splits[1], (BASELINE_COUNT, 2), 0, STATION_COUNT), jax.random.fold_in(splits[1], 1), 0, STATION_COUNT - 1).astype(jnp.int32)
    station_coords = jnp.clip(jax.random.uniform(splits[2], (STATION_COUNT, 2), jnp.float32, -1.0, 1.0), -1.0, 1.0)
    dir_lm = jnp.clip(jax.random.uniform(splits[3], (DIRS, 2), jnp.float32, -0.5, 0.5), -0.5, 0.5)
    time_beam = noise(splits[4], (DIRS, TIME_SAMPLES), 1.0, 6.0, (), jnp.float32)
    dir_cluster = draw_dir_cluster(jax.random.fold_in(splits[7], 71), 0)
    seed_block = set_ends(jax.random.randint(splits[6], (TILES, TIME_SAMPLES, RANK), -8, 9), jax.random.fold_in(splits[6], 1), -8, 8).astype(jnp.int32)
    return dict(vis=vis, station_pair_index=station_pair_index, station_coords=station_coords, dir_lm=dir_lm, time_beam=time_beam, dir_cluster=dir_cluster, seed_block=seed_block)


HIGHEST = lax.Precision.HIGHEST
PHASE_SCALE = 20.0
RHO_SCALE = 0.5

def orthonormal(block):
    square = jnp.dot(block.T, block, precision=HIGHEST)
    lower = jnp.linalg.cholesky(square)
    solved = jax.scipy.linalg.solve_triangular(lower, block.T, lower=True)
    return solved.T

def beam_fit(beam_proj, basis, time_beam):
    coeffs = jnp.dot(beam_proj, basis, precision=HIGHEST)
    inner = beam_proj - jnp.dot(coeffs, basis.T, precision=HIGHEST)
    return lax.optimization_barrier(jnp.sum(inner * time_beam, axis=-1))

def reference(vis, station_pair_index, station_coords, dir_lm, time_beam, dir_cluster, seed_block):
    uv = station_coords[station_pair_index[:, 0]] - station_coords[station_pair_index[:, 1]]
    geo = jnp.dot(dir_lm, uv.T, precision=HIGHEST)
    chan = jnp.arange(CHANNEL_COUNT).astype(jnp.float32)
    freq = 1.0 + chan / CHANNEL_COUNT
    phase = (PHASE_SCALE * freq)[None, :, None] * geo[:, None, :]
    response = jnp.stack([jnp.cos(phase), jnp.sin(phase)], axis=1).astype(jnp.bfloat16)

    def tile_work(index):
        start = (index * TILE).astype(jnp.int32)
        vis_tile = lax.dynamic_slice_in_dim(vis, start, TILE, 2).astype(jnp.float32)
        resp_tile = lax.dynamic_slice_in_dim(response, start, TILE, 3).astype(jnp.float32)
        gram = jnp.einsum('pcbt,pcbs->ts', vis_tile, vis_tile, precision=HIGHEST)
        beam_proj = jnp.einsum('dpcb,pcbt->dt', resp_tile, vis_tile, precision=HIGHEST)
        model_gram = jnp.einsum('dpcb,epcb->de', resp_tile, resp_tile, precision=HIGHEST)
        block = lax.dynamic_index_in_dim(seed_block, index, 0, keepdims=False).astype(jnp.float32)
        for step in range(SUB_ITERS):
            block = orthonormal(jnp.dot(gram, block, precision=HIGHEST))
        basis = block.astype(jnp.bfloat16).astype(jnp.float32)
        proj = jnp.einsum('pcbt,tk->pcbk', vis_tile, basis, precision=HIGHEST)
        correction = jnp.einsum('pcbk,tk->pcbt', proj, basis, precision=HIGHEST)
        filtered_visibility = (vis_tile - correction).astype(jnp.bfloat16)
        rhs_dir = beam_fit(beam_proj, basis, time_beam)
        return (filtered_visibility, rhs_dir, model_gram)
    filtered_visibility, rhs_dir, model_gram = lax.map(tile_work, jnp.arange(TILES).astype(jnp.int32))
    clean = jnp.transpose(filtered_visibility, (1, 2, 0, 3, 4)).reshape(2, CHANNEL_COUNT, BASELINE_COUNT, TIME_SAMPLES)
    beam_gram = jnp.dot(time_beam, time_beam.T, precision=HIGHEST)
    member = (dir_cluster[:, None] == jnp.arange(CL)[None, :]).astype(jnp.float32)
    weighted = model_gram * beam_gram[None]
    normal_matrix = jnp.einsum('dk,jde->jke', member, weighted, precision=HIGHEST)
    normal_matrix = jnp.einsum('jke,el->jkl', normal_matrix, member, precision=HIGHEST)
    rhs = jnp.einsum('dk,jd->jk', member, rhs_dir, precision=HIGHEST)
    rho = RHO_SCALE * jnp.trace(normal_matrix, axis1=1, axis2=2) / CL
    system = normal_matrix + rho[:, None, None] * jnp.eye(CL, dtype=jnp.float32)[None]
    lower = jnp.linalg.cholesky(system)
    center = jnp.zeros((CL,), jnp.float32)
    dual = jnp.zeros((TILES, CL), jnp.float32)
    solved = jnp.zeros((TILES, CL), jnp.float32)
    for step in range(ADMM_ITERS):
        target = rhs + rho[:, None] * (center[None, :] - dual)
        solved = jax.scipy.linalg.cho_solve((lower, True), target[..., None])[..., 0]
        center = lax.optimization_barrier(jnp.sum(solved + dual, axis=0)) / TILES
        dual = dual + solved - center[None, :]
    factor = jnp.sqrt(jnp.float32(CHANNEL_COUNT * TILE * TIME_SAMPLES))
    return (clean, solved * factor, center * factor)
```

```python
import functools

import jax
import jax.numpy as jnp
from jax import lax
from jax.experimental import pallas as pl
from jax.experimental.pallas import tpu as pltpu
from jax.sharding import PartitionSpec as P

CL = 12
SUB_ITERS = 3
ADMM_ITERS = 6
PHASE_SCALE = 20.0
RHO_SCALE = 0.5

HIGHEST = lax.Precision.HIGHEST
MESH = pl.DeviceIdType.MESH
F32 = jnp.float32
BF16 = jnp.bfloat16
LANES = 128
GROUP = 16
NT = (((1,), (1,)), ((), ()))
TN = (((0,), (0,)), ((), ()))


def split3(x):
    a = x.astype(BF16).astype(F32)
    rest = x - a
    b = rest.astype(BF16).astype(F32)
    return a, b, rest - b


def sincos(phase):
    k = jnp.floor(phase * F32(0.6366197723675814) + F32(0.5))
    r = phase - k * F32(1.5703125)
    r = r - k * F32(4.837512969970703125e-4)
    r = r - k * F32(7.54978995489188216e-8)
    r2 = r * r
    s = r + r * r2 * (F32(-1.6666654611e-1) + r2 * (F32(8.3321608736e-3) + r2 * F32(-1.9515295891e-4)))
    c = (F32(1.0) - F32(0.5) * r2) + r2 * r2 * (
        F32(4.166664568298827e-2) + r2 * (F32(-1.388731625493765e-3) + r2 * F32(2.443315711809948e-5))
    )
    ki = k.astype(jnp.int32)
    odd = (ki & 1) == 1
    cos = jnp.where(odd, s, c)
    sin = jnp.where(odd, c, s)
    cos = jnp.where(((ki + 1) & 2) == 2, -cos, cos)
    sin = jnp.where((ki & 2) == 2, -sin, sin)
    return cos, sin


def orthonormal(rows):
    count = rows.shape[1]
    sub = lax.broadcasted_iota(jnp.int32, (1, count, 1), 1)
    for k in range(0, count, 2):
        lead = rows[:, k : k + 1, :]
        follow = rows[:, k + 1 : k + 2, :]
        dots = jnp.sum(rows * lead, axis=-1, keepdims=True)
        others = jnp.sum(rows * follow, axis=-1, keepdims=True)
        ratio = dots / dots[:, k : k + 1, :]
        mix = ratio[:, k + 1 : k + 2, :]
        follow = follow - mix * lead
        others = others - mix * dots
        coef = jnp.where(sub > k, ratio, F32(0.0))
        coef_follow = jnp.where(sub > k + 1, others / others[:, k + 1 : k + 2, :], F32(0.0))
        rows = rows - coef * lead - coef_follow * follow
    norm = jnp.sum(rows * rows, axis=-1, keepdims=True)
    return rows / jnp.sqrt(norm)


def main_kernel(
    n_chan, n_bl, channels,
    vis_hbm, pair_hbm, coords_hbm, lm_hbm, tb_hbm, cluster_hbm, seed_hbm,
    clean_ref, gains_ref, cons_ref,
    vis_ref, pair_ref, coords_ref, lm_ref, tb_ref, cluster_ref, seed_ref,
    gsplit, resp, lmp, tbp, clp, coord_rows, uv_ref, bsplit, tsplit, qsplit, before_ref,
    ybuf, nbuf, mbuf, vbuf, lbuf, send_sems, recv_sems, vis_sems, load_sems,
):
    chan_dev, base_dev, times = vis_ref.shape[1:]
    tiles, rank = seed_ref.shape[0], seed_ref.shape[1]
    tile = base_dev // tiles
    dirs = tb_ref.shape[0]
    dpad = tbp.shape[0]
    stations = coords_ref.shape[1]
    n_all = n_chan * n_bl
    tiles_all = tiles * n_bl
    my_chan = lax.axis_index("chan")
    my_bl = lax.axis_index("bl")
    my_id = my_chan * n_bl + my_bl

    loads = [
        pltpu.make_async_copy(src, dst, load_sems.at[i])
        for i, (src, dst) in enumerate(
            (
                (seed_hbm, seed_ref),
                (pair_hbm, pair_ref),
                (coords_hbm, coords_ref),
                (lm_hbm, lm_ref),
                (tb_hbm, tb_ref),
                (cluster_hbm, cluster_ref),
            )
        )
    ]
    vis_loads = []
    for j in range(tiles):
        at = (slice(None), slice(None), pl.ds(j * tile, tile), slice(None))
        vis_loads.append(pltpu.make_async_copy(vis_hbm.at[at], vis_ref.at[at], vis_sems.at[j]))
    loads[0].start()
    for load in vis_loads:
        load.start()
    for load in loads[1:]:
        load.start()

    def everyone(off):
        other = lax.rem(my_id + off, n_all)
        return (lax.div(other, n_bl), lax.rem(other, n_bl))

    def along_chan(off):
        return (lax.rem(my_chan + off, n_chan), my_bl)

    def along_bl(off):
        return (my_chan, lax.rem(my_bl + off, n_bl))

    barrier = pltpu.get_barrier_semaphore()

    @pl.loop(1, n_all)
    def _(off):
        pl.semaphore_signal(barrier, inc=1, device_id=everyone(off), device_id_type=MESH)

    def push(buf, me, n, peer, phase):
        @pl.loop(1, n)
        def _(off):
            pltpu.make_async_remote_copy(
                src_ref=buf.at[me],
                dst_ref=buf.at[me],
                send_sem=send_sems.at[phase],
                recv_sem=recv_sems.at[phase],
                device_id=peer(off),
                device_id_type=MESH,
            ).start()

    def arrived(buf, n, phase):
        part = buf.at[pl.ds(0, n - 1)]
        pltpu.make_async_copy(part, part, recv_sems.at[phase]).wait()

    def sent(buf, n, phase):
        part = buf.at[pl.ds(0, n - 1)]
        pltpu.make_async_copy(part, part, send_sems.at[phase]).wait()

    def total(buf, n):
        out = buf[0]
        for i in range(1, n):
            out = out + buf[i]
        return out

    def vis_tile(j):
        return vis_ref[:, :, j * tile : (j + 1) * tile, :].reshape(2 * chan_dev * tile, times)

    first = []
    loads[0].wait()
    for j in range(tiles):
        vis_loads[j].wait()
        v = vis_tile(j)
        seed = seed_ref[j].astype(F32)
        seed = jnp.concatenate([seed, jnp.zeros_like(seed)], axis=0).astype(BF16)
        p1, p2, p3 = split3(lax.dot_general(seed, v, NT, preferred_element_type=F32)[:rank])
        lhs = jnp.concatenate([p1, p2, p3, jnp.zeros_like(p1)], axis=0).astype(BF16)
        acc = jnp.dot(lhs, v, preferred_element_type=F32)
        first.append(acc[:rank] + (acc[rank : 2 * rank] + acc[2 * rank : 3 * rank]))
    ybuf[0, my_chan] = jnp.concatenate(first, axis=0)
    pl.semaphore_wait(barrier, n_all - 1)
    push(ybuf.at[0], my_chan, n_chan, along_chan, 0)

    for j in range(tiles):
        v = vis_tile(j)
        gram = lax.dot_general(v, v, TN, preferred_element_type=F32)
        g1, g2, g3 = split3(gram)
        gsplit[j, 0] = g1.astype(BF16)
        gsplit[j, 1] = g2.astype(BF16)
        gsplit[j, 2] = g3.astype(BF16)

    for load in loads[1:]:
        load.wait()
    lmp[...] = jnp.zeros_like(lmp)
    lmp[0:2, 0:dirs] = lm_ref[...]
    tbp[...] = jnp.zeros_like(tbp)
    tbp[0:dirs, :] = tb_ref[...]
    clp[...] = jnp.full_like(clp, -1)
    clp[0:1, 0:dirs] = cluster_ref[...]
    c1, c2, c3 = split3(coords_ref[...])
    coord_rows[...] = jnp.zeros_like(coord_rows)
    coord_rows[0:2, :] = c1
    coord_rows[2:4, :] = c2
    coord_rows[4:6, :] = c3
    tb = tbp[...]
    beam_gram = lax.dot_general(tb, tb, NT, precision=HIGHEST, preferred_element_type=F32)
    member = jnp.where(
        lax.broadcasted_iota(jnp.int32, (LANES, dpad), 0) == clp[0:1, 0:dpad], F32(1.0), F32(0.0)
    )
    station = lax.broadcasted_iota(jnp.int32, (stations, base_dev), 0)
    pick = jnp.where(station == pair_ref[0:1, :], F32(1.0), F32(0.0)) - jnp.where(
        station == pair_ref[1:2, :], F32(1.0), F32(0.0)
    )
    uv_ref[...] = jnp.dot(coord_rows[...].astype(BF16), pick.astype(BF16), preferred_element_type=F32)
    uv = uv_ref[0:2, :] + uv_ref[2:4, :] + uv_ref[4:6, :]
    uv_ref[0:2, :] = uv
    uv_ref[2:8, :] = jnp.zeros((6, base_dev), F32)
    geo = lax.dot_general(
        lmp[:, 0:dpad], uv_ref[0:8, :], TN, precision=HIGHEST, preferred_element_type=F32
    )
    for c in range(chan_dev):
        chan = jnp.full((1, tile), my_chan * chan_dev + c, jnp.int32).astype(F32)
        scale = F32(PHASE_SCALE) * (F32(1.0) + chan / F32(channels))
        for j in range(tiles):
            cos, sin = sincos(scale * geo[:, j * tile : (j + 1) * tile])
            resp[j, :, c * tile : (c + 1) * tile] = cos.astype(BF16)
            resp[j, :, (chan_dev + c) * tile : (chan_dev + c + 1) * tile] = sin.astype(BF16)

    def advance(block, step):
        parts = []
        for j in range(tiles):
            z1, z2, z3 = split3(block[j])
            lhs = jnp.concatenate([z1, z2, z3, jnp.zeros_like(z1)], axis=0).astype(BF16)
            p1 = jnp.dot(lhs, gsplit[j, 0], preferred_element_type=F32)
            p2 = jnp.dot(lhs, gsplit[j, 1], preferred_element_type=F32)
            p3 = jnp.dot(lhs, gsplit[j, 2], preferred_element_type=F32)
            low = p1[2 * rank : 3 * rank] + p2[rank : 2 * rank] + p3[:rank]
            parts.append(p1[:rank] + (p1[rank : 2 * rank] + p2[:rank] + low))
        ybuf[step, my_chan] = jnp.concatenate(parts, axis=0)
        push(ybuf.at[step], my_chan, n_chan, along_chan, step)

    def gathered(step):
        arrived(ybuf.at[step], n_chan, step)
        return orthonormal(total(ybuf.at[step], n_chan).reshape(tiles, rank, times))

    advance(gathered(0), 1)

    member_rows = member[0:GROUP]
    halves = []
    for j in range(tiles):
        r = resp[j]
        model = lax.dot_general(r, r, NT, preferred_element_type=F32)
        halves.append(jnp.dot(member_rows, model * beam_gram, precision=HIGHEST, preferred_element_type=F32))
    half = jnp.concatenate(halves, axis=0)
    nbuf[my_chan] = lax.dot_general(half, member, NT, precision=HIGHEST, preferred_element_type=F32)
    push(nbuf, my_chan, n_chan, along_chan, SUB_ITERS)
    weighted = []
    for j in range(tiles):
        at = slice(j * dpad, (j + 1) * dpad)
        bp = jnp.dot(resp[j], vis_tile(j), preferred_element_type=F32)
        weighted.append(bp * tb)
        for ref, part in ((bsplit, bp), (tsplit, tb)):
            b1, b2, b3 = split3(part)
            ref[0, at] = b1.astype(BF16)
            ref[1, at] = b2.astype(BF16)
            ref[2, at] = b3.astype(BF16)
    before_ref[...] = lax.dot_general(
        jnp.ones((8, times), F32), jnp.concatenate(weighted, axis=0), NT, precision=HIGHEST, preferred_element_type=F32
    )
    advance(gathered(1), 2)

    arrived(nbuf, n_chan, SUB_ITERS)
    normal = total(nbuf, n_chan)
    sub = lax.broadcasted_iota(jnp.int32, (GROUP, LANES), 0)
    lane = lax.broadcasted_iota(jnp.int32, (GROUP, LANES), 1)
    eye = jnp.where(sub == lane, F32(1.0), F32(0.0))
    inv, inv_rho = [], []
    for j in range(tiles):
        mat = normal[j * GROUP : (j + 1) * GROUP]
        trace = jnp.sum(jnp.sum(mat * eye, axis=1, keepdims=True), axis=0, keepdims=True)
        recip = F32(1.0) / (F32(RHO_SCALE) * trace / F32(CL))
        inv_rho.append(recip)
        inv.append(mat * recip + eye)
    for p in range(CL):
        for j in range(tiles):
            mat = inv[j]
            col = mat[:, p : p + 1]
            row = mat[p : p + 1, :]
            d = F32(1.0) / mat[p : p + 1, p : p + 1]
            row = jnp.where(lane[0:1] == p, d, row * d)
            mat = jnp.where(lane == p, F32(0.0), mat)
            inv[j] = jnp.where(sub == p, row, mat - col * row)
    big = []
    for j in range(tiles):
        e = eye - inv[j]
        if j:
            e = pltpu.roll(e, j * GROUP, 1)
        big.append(e)
    pad = jnp.zeros((LANES - tiles * GROUP, LANES), F32)
    e1 = jnp.concatenate(big + [pad], axis=0)

    def times_of(a, b):
        return jnp.dot(a, b, precision=HIGHEST, preferred_element_type=F32)

    def fold(m):
        out = m[0:GROUP]
        for j in range(1, tiles):
            out = out + m[j * GROUP : (j + 1) * GROUP]
        return out

    e2 = times_of(e1, e1)
    e3 = times_of(e2, e1)
    e4 = times_of(e2, e2)
    e5 = times_of(e2, e3)
    e6 = times_of(e3, e3)
    powers = [fold(m) for m in (e1, e2, e3, e4, e5, e6)]
    group = lax.div(lane, GROUP)
    by_tile = []
    for j in range(tiles):
        out = jnp.zeros((GROUP, LANES), F32)
        for p in range(ADMM_ITERS):
            shift = (p - j) * GROUP % LANES
            m = pltpu.roll(powers[p], shift, 1) if shift else powers[p]
            out = jnp.where(group == p, m, out)
        by_tile.append(out)
    packed = by_tile[0]
    for j in range(1, tiles):
        packed = packed + by_tile[j]
    mbuf[my_bl] = packed
    push(mbuf, my_bl, n_bl, along_bl, SUB_ITERS + 1)
    eye_all = jnp.where(lax.rem(lane, GROUP) == sub, F32(1.0), F32(0.0))
    eye_all = jnp.where(lane < tiles * GROUP, eye_all, F32(0.0))
    powers = [eye_all] + powers

    eye_rep = jnp.where((lax.rem(lane, GROUP) == sub) & (group < ADMM_ITERS), F32(1.0), F32(0.0))
    final = powers[ADMM_ITERS - 1] - powers[ADMM_ITERS]
    for j in range(tiles):
        own = jnp.where(group == j, final, F32(0.0))
        both = jnp.concatenate([eye_rep - by_tile[j], own], axis=1) * inv_rho[j]
        q1, q2, q3 = split3(
            lax.dot_general(member_rows, both, TN, precision=HIGHEST, preferred_element_type=F32)
        )
        at = slice(j * dpad, (j + 1) * dpad)
        qsplit[0, at] = q1.astype(BF16)
        qsplit[1, at] = q2.astype(BF16)
        qsplit[2, at] = q3.astype(BF16)

    def stacked(row):
        a, b, c = split3(row)
        at = lax.broadcasted_iota(jnp.int32, (16, row.shape[1]), 0)
        return jnp.where(at == 0, a, jnp.where(at == 1, b, jnp.where(at == 2, c, F32(0.0)))).astype(BF16)

    def row_times(row, parts):
        lhs = stacked(row)
        at = lax.broadcasted_iota(jnp.int32, (16, parts[0].shape[1]), 0)
        acc = jnp.where(at < 1, jnp.dot(lhs, parts[2], preferred_element_type=F32), F32(0.0))
        acc = acc + jnp.where(at < 2, jnp.dot(lhs, parts[1], preferred_element_type=F32), F32(0.0))
        acc = acc + jnp.where(at < 3, jnp.dot(lhs, parts[0], preferred_element_type=F32), F32(0.0))
        return jnp.sum(acc, axis=0, keepdims=True)

    def along_times(lhs, ref):
        acc = lax.dot_general(lhs, ref[2], NT, preferred_element_type=F32)
        acc = acc + lax.dot_general(lhs, ref[1], NT, preferred_element_type=F32)
        return acc + lax.dot_general(lhs, ref[0], NT, preferred_element_type=F32)

    basis = gathered(2).astype(BF16).astype(F32).reshape(tiles * rank, times)
    rows16 = basis.astype(BF16)
    product = along_times(rows16, bsplit) * along_times(rows16, tsplit)
    row_tile = lax.div(lax.broadcasted_iota(jnp.int32, product.shape, 0), rank)
    lane_tile = lax.div(lax.broadcasted_iota(jnp.int32, product.shape, 1), dpad)
    product = jnp.where(row_tile == lane_tile, product, F32(0.0))
    rhs_row = before_ref[0:1] - jnp.sum(product, axis=0, keepdims=True)
    row = row_times(rhs_row, (qsplit[0], qsplit[1], qsplit[2]))
    vbuf[my_id] = row[:, 0:LANES]
    lbuf[my_chan] = row[:, LANES : 2 * LANES]
    push(vbuf, my_id, n_all, everyone, SUB_ITERS + 2)
    push(lbuf, my_chan, n_chan, along_chan, SUB_ITERS + 3)

    part_lane = lax.broadcasted_iota(jnp.int32, (1, 4 * rank), 1)
    for j in range(tiles):
        own = basis[j * rank : (j + 1) * rank]
        wide = jnp.concatenate([own, own, own, jnp.zeros_like(own)], axis=0).astype(BF16)
        v = vis_tile(j)
        proj = lax.dot_general(v, wide, NT, preferred_element_type=F32)
        a, b, c = split3(proj)
        parts = jnp.where(part_lane < rank, a, jnp.where(part_lane < 2 * rank, b, c)).astype(BF16)
        correction = jnp.dot(parts, wide, preferred_element_type=F32)
        clean_ref[:, :, j * tile : (j + 1) * tile, :] = (
            (v.astype(F32) - correction).astype(BF16).reshape(2, chan_dev, tile, times)
        )

    arrived(mbuf, n_bl, SUB_ITERS + 1)
    moments = jnp.where(group < ADMM_ITERS - 1, total(mbuf, n_bl) * F32(1.0 / tiles_all), F32(0.0))
    history = jnp.where(group == 0, eye, pltpu.roll(moments, GROUP, 1))
    gain = jnp.where(group < ADMM_ITERS - 1, history, F32(0.0)) - F32(2.0) * moments
    local = []
    for i in range(1, ADMM_ITERS - 1):
        k = ADMM_ITERS - 2 - i
        local.append(F32(3.0) * powers[k + 1] - powers[k] - F32(2.0) * powers[k + 2])
    local.append(F32(2.0) * (powers[0] - powers[1]))
    apply = [jnp.where(lane == sub + tiles * GROUP, F32(1.0), F32(0.0))]
    for k in range(ADMM_ITERS - 2, -1, -1):
        pad = jnp.zeros((LANES - len(apply) * GROUP, LANES), F32)
        apply.insert(0, local[k] + times_of(gain, jnp.concatenate(apply + [pad], axis=0)))
    factor = F32((channels * tile * times) ** 0.5)
    pad = jnp.zeros((LANES - len(apply) * GROUP, LANES), F32)
    apply = jnp.concatenate(apply + [pad], axis=0) * F32((channels * tile * times) ** 0.5 / tiles_all)
    parts = tuple(part.astype(BF16) for part in split3(apply))
    arrived(vbuf, n_all, SUB_ITERS + 2)
    arrived(lbuf, n_chan, SUB_ITERS + 3)
    x = row_times(total(vbuf, n_all), parts) + total(lbuf, n_chan) * factor
    x = jnp.broadcast_to(x, (8, LANES))
    for j in range(tiles):
        at = x if j == 0 else pltpu.roll(x, LANES - j * GROUP, 1)
        gains_ref[j : j + 1, :] = at[0:1, 0:CL]
    cons_ref[...] = pltpu.roll(x, LANES - tiles * GROUP, 1)[0:1, 0:CL]

    for step in range(SUB_ITERS):
        sent(ybuf.at[step], n_chan, step)
    sent(nbuf, n_chan, SUB_ITERS)
    sent(mbuf, n_bl, SUB_ITERS + 1)
    sent(vbuf, n_all, SUB_ITERS + 2)
    sent(lbuf, n_chan, SUB_ITERS + 3)


def store_kernel(clean_in, gains_in, cons_in, clean_out, gains_out, cons_out, sems):
    parts, chans = clean_in.shape[:2]
    stores = [
        pltpu.make_async_copy(gains_in, gains_out, sems.at[0]),
        pltpu.make_async_copy(cons_in, cons_out, sems.at[1]),
    ]
    for p in range(parts):
        for c in range(chans):
            stores.append(
                pltpu.make_async_copy(clean_in.at[p, c], clean_out.at[p, c], sems.at[2 + p * chans + c])
            )
    for store in stores:
        store.start()
    for store in stores:
        store.wait()


def per_device(vis, station_pair_index, station_coords, dir_lm, time_beam, dir_cluster, seed_block):
    n_chan = lax.axis_size("chan")
    n_bl = lax.axis_size("bl")
    chan_dev, base_dev, times = vis.shape[1:]
    tiles, _, rank = seed_block.shape
    tile = base_dev // tiles
    dirs = dir_lm.shape[0]
    dpad = (dirs + 15) // 16 * 16
    stations = station_coords.shape[0]
    vmem = pl.BlockSpec(memory_space=pltpu.VMEM)
    anywhere = pl.BlockSpec(memory_space=pl.ANY)
    shapes = (
        jax.ShapeDtypeStruct(vis.shape, BF16),
        jax.ShapeDtypeStruct((tiles, CL), F32),
        jax.ShapeDtypeStruct((1, CL), F32),
    )
    results = pl.pallas_call(
        functools.partial(main_kernel, n_chan, n_bl, chan_dev * n_chan),
        out_shape=tuple(pltpu.VMEM(s.shape, s.dtype) for s in shapes),
        in_specs=[anywhere] * 7,
        out_specs=(vmem, vmem, vmem),
        scratch_shapes=[
            pltpu.VMEM(vis.shape, BF16),
            pltpu.VMEM((2, base_dev), jnp.int32),
            pltpu.VMEM((2, stations), F32),
            pltpu.VMEM((2, dirs), F32),
            pltpu.VMEM((dirs, times), F32),
            pltpu.VMEM((1, dirs), jnp.int32),
            pltpu.VMEM((tiles, rank, times), jnp.int32),
            pltpu.VMEM((tiles, 3, times, times), BF16),
            pltpu.VMEM((tiles, dpad, 2 * chan_dev * tile), BF16),
            pltpu.VMEM((8, LANES), F32),
            pltpu.VMEM((dpad, times), F32),
            pltpu.VMEM((8, LANES), jnp.int32),
            pltpu.VMEM((GROUP, stations), F32),
            pltpu.VMEM((GROUP, base_dev), F32),
            pltpu.VMEM((3, tiles * dpad, times), BF16),
            pltpu.VMEM((3, tiles * dpad, times), BF16),
            pltpu.VMEM((3, tiles * dpad, 2 * LANES), BF16),
            pltpu.VMEM((8, tiles * dpad), F32),
            pltpu.VMEM((SUB_ITERS, n_chan, tiles * rank, times), F32),
            pltpu.VMEM((n_chan, tiles * GROUP, LANES), F32),
            pltpu.VMEM((n_bl, GROUP, LANES), F32),
            pltpu.VMEM((n_chan * n_bl, 1, LANES), F32),
            pltpu.VMEM((n_chan, 1, LANES), F32),
            pltpu.SemaphoreType.DMA((SUB_ITERS + 4,)),
            pltpu.SemaphoreType.DMA((SUB_ITERS + 4,)),
            pltpu.SemaphoreType.DMA((tiles,)),
            pltpu.SemaphoreType.DMA((6,)),
        ],
        compiler_params=pltpu.CompilerParams(
            collective_id=0, has_side_effects=True, vmem_limit_bytes=32 * 1024 * 1024
        ),
    )(
        *(
            pltpu.with_memory_space_constraint(a, pltpu.HBM)
            for a in (
                vis,
                station_pair_index.T,
                station_coords.T,
                dir_lm.T,
                time_beam,
                dir_cluster.reshape(1, dirs),
                jnp.swapaxes(seed_block, 1, 2),
            )
        )
    )
    clean, gains, consensus = pl.pallas_call(
        store_kernel,
        out_shape=shapes,
        in_specs=[vmem] * 3,
        out_specs=(anywhere, anywhere, anywhere),
        scratch_shapes=[pltpu.SemaphoreType.DMA((2 + 2 * chan_dev,))],
        compiler_params=pltpu.CompilerParams(vmem_limit_bytes=8 * 1024 * 1024),
    )(*results)
    return clean, gains, consensus.reshape(CL)


def solution(mesh):
    placed = (P(None, "chan", "bl", None), P("bl", None), P(), P(), P(), P(), P("bl", None, None))
    return jax.shard_map(
        per_device,
        mesh=mesh,
        in_specs=placed,
        out_specs=(P(None, "chan", "bl", None), P("bl", None), P()),
        check_vma=False,
    )
```

```python
import functools

import jax
import jax.numpy as jnp
from jax import lax
from jax.experimental import pallas as pl
from jax.experimental.pallas import tpu as pltpu
from jax.sharding import PartitionSpec as P

CL = 12
SUB_ITERS = 3
ADMM_ITERS = 6
PHASE_SCALE = 20.0
RHO_SCALE = 0.5

HIGHEST = lax.Precision.HIGHEST
MESH = pl.DeviceIdType.MESH
F32 = jnp.float32
BF16 = jnp.bfloat16
LANES = 128
GROUP = 16
NT = (((1,), (1,)), ((), ()))
TN = (((0,), (0,)), ((), ()))


def split3(x):
    a = x.astype(BF16).astype(F32)
    rest = x - a
    b = rest.astype(BF16).astype(F32)
    return a, b, rest - b


def sincos(phase):
    k = jnp.floor(phase * F32(0.6366197723675814) + F32(0.5))
    r = phase - k * F32(1.5703125)
    r = r - k * F32(4.837512969970703125e-4)
    r = r - k * F32(7.54978995489188216e-8)
    r2 = r * r
    s = r + r * r2 * (F32(-1.6666654611e-1) + r2 * (F32(8.3321608736e-3) + r2 * F32(-1.9515295891e-4)))
    c = (F32(1.0) - F32(0.5) * r2) + r2 * r2 * (
        F32(4.166664568298827e-2) + r2 * (F32(-1.388731625493765e-3) + r2 * F32(2.443315711809948e-5))
    )
    ki = k.astype(jnp.int32)
    odd = (ki & 1) == 1
    cos = jnp.where(odd, s, c)
    sin = jnp.where(odd, c, s)
    cos = jnp.where(((ki + 1) & 2) == 2, -cos, cos)
    sin = jnp.where((ki & 2) == 2, -sin, sin)
    return cos, sin


def orthonormal(rows):
    count = rows.shape[1]
    sub = lax.broadcasted_iota(jnp.int32, (1, count, 1), 1)
    cols = [jnp.sum(rows * rows[:, k : k + 1, :], axis=-1, keepdims=True) for k in range(count)]
    square = cols[0][:, 0:1, :]
    for k in range(count):
        pivot = cols[k][:, k : k + 1, :]
        square = jnp.where(sub == k, pivot, square)
        if k == count - 1:
            break
        ratio = jnp.where(sub > k, cols[k] * (F32(1.0) / pivot), F32(0.0))
        for m in range(k + 1, count):
            cols[m] = cols[m] - ratio * cols[m][:, k : k + 1, :]
        rows = rows - ratio * rows[:, k : k + 1, :]
    return rows * lax.rsqrt(square)


def main_kernel(
    n_chan, n_bl, channels,
    vis_hbm, pair_hbm, coords_hbm, lm_hbm, tb_hbm, cluster_hbm, seed_hbm,
    clean_ref, gains_ref, cons_ref,
    vis_ref, pair_ref, coords_ref, lm_ref, tb_ref, cluster_ref, seed_ref,
    gsplit, resp, lmp, tbp, clp, coord_rows, uv_ref, bsplit, tsplit, qsplit, before_ref, spread,
    ybuf, nbuf, mbuf, vbuf, lbuf, send_sems, recv_sems, vis_sems, load_sems,
):
    chan_dev, base_dev, times = vis_ref.shape[1:]
    tiles, rank = seed_ref.shape[0], seed_ref.shape[1]
    tile = base_dev // tiles
    dirs = tb_ref.shape[0]
    dpad = tbp.shape[0]
    stations = coords_ref.shape[1]
    n_all = n_chan * n_bl
    tiles_all = tiles * n_bl
    my_chan = lax.axis_index("chan")
    my_bl = lax.axis_index("bl")
    my_id = my_chan * n_bl + my_bl

    loads = [
        pltpu.make_async_copy(src, dst, load_sems.at[i])
        for i, (src, dst) in enumerate(
            (
                (seed_hbm, seed_ref),
                (pair_hbm, pair_ref),
                (coords_hbm, coords_ref),
                (lm_hbm, lm_ref),
                (tb_hbm, tb_ref),
                (cluster_hbm, cluster_ref),
            )
        )
    ]
    vis_loads = []
    for j in range(tiles):
        at = (slice(None), slice(None), pl.ds(j * tile, tile), slice(None))
        vis_loads.append(pltpu.make_async_copy(vis_hbm.at[at], vis_ref.at[at], vis_sems.at[j]))
    loads[0].start()
    for load in vis_loads:
        load.start()
    for load in loads[1:]:
        load.start()

    def everyone(off):
        other = lax.rem(my_id + off, n_all)
        return (lax.div(other, n_bl), lax.rem(other, n_bl))

    def along_chan(off):
        return (lax.rem(my_chan + off, n_chan), my_bl)

    def along_bl(off):
        return (my_chan, lax.rem(my_bl + off, n_bl))

    barrier = pltpu.get_barrier_semaphore()

    @pl.loop(1, n_all)
    def _(off):
        pl.semaphore_signal(barrier, inc=1, device_id=everyone(off), device_id_type=MESH)

    def push(buf, me, n, peer, phase):
        @pl.loop(1, n)
        def _(off):
            pltpu.make_async_remote_copy(
                src_ref=buf.at[me],
                dst_ref=buf.at[me],
                send_sem=send_sems.at[phase],
                recv_sem=recv_sems.at[phase],
                device_id=peer(off),
                device_id_type=MESH,
            ).start()

    def arrived(buf, n, phase):
        part = buf.at[pl.ds(0, n - 1)]
        pltpu.make_async_copy(part, part, recv_sems.at[phase]).wait()

    def sent(buf, n, phase):
        part = buf.at[pl.ds(0, n - 1)]
        pltpu.make_async_copy(part, part, send_sems.at[phase]).wait()

    def total(buf, n):
        out = buf[0]
        for i in range(1, n):
            out = out + buf[i]
        return out

    def vis_tile(j):
        return vis_ref[:, :, j * tile : (j + 1) * tile, :].reshape(2 * chan_dev * tile, times)

    first = []
    loads[0].wait()
    for j in range(tiles):
        vis_loads[j].wait()
        v = vis_tile(j)
        seed = seed_ref[j].astype(F32)
        seed = jnp.concatenate([seed, jnp.zeros_like(seed)], axis=0).astype(BF16)
        p1, p2, p3 = split3(lax.dot_general(seed, v, NT, preferred_element_type=F32)[:rank])
        lhs = jnp.concatenate([p1, p2, p3, jnp.zeros_like(p1)], axis=0).astype(BF16)
        acc = jnp.dot(lhs, v, preferred_element_type=F32)
        first.append(acc[:rank] + (acc[rank : 2 * rank] + acc[2 * rank : 3 * rank]))
    ybuf[0, my_chan] = jnp.concatenate(first, axis=0)
    pl.semaphore_wait(barrier, n_all - 1)
    push(ybuf.at[0], my_chan, n_chan, along_chan, 0)

    for load in loads[1:]:
        load.wait()
    lmp[...] = jnp.zeros_like(lmp)
    lmp[0:2, 0:dirs] = lm_ref[...]
    tbp[...] = jnp.zeros_like(tbp)
    tbp[0:dirs, :] = tb_ref[...]
    clp[...] = jnp.full_like(clp, -1)
    clp[0:1, 0:dirs] = cluster_ref[...]
    c1, c2, c3 = split3(coords_ref[...])
    coord_rows[...] = jnp.zeros_like(coord_rows)
    coord_rows[0:2, :] = c1
    coord_rows[2:4, :] = c2
    coord_rows[4:6, :] = c3
    tb = tbp[...]
    beam_gram = lax.dot_general(tb, tb, NT, precision=HIGHEST, preferred_element_type=F32)
    member = jnp.where(
        lax.broadcasted_iota(jnp.int32, (LANES, dpad), 0) == clp[0:1, 0:dpad], F32(1.0), F32(0.0)
    )
    named = jnp.broadcast_to(clp[0:1, :].astype(F32), (LANES, LANES)).T[0:dpad]
    lane_group = lax.rem(lax.div(lax.broadcasted_iota(jnp.int32, (dpad, LANES), 1), GROUP), tiles)
    for m in range(CL):
        hit = jnp.where(named == F32(m), F32(1.0), F32(0.0))
        for j in range(tiles):
            spread[j * dpad : (j + 1) * dpad, m * LANES : (m + 1) * LANES] = jnp.where(
                lane_group == j, hit, F32(0.0)
            ).astype(BF16)
    station = lax.broadcasted_iota(jnp.int32, (stations, base_dev), 0)
    pick = jnp.where(station == pair_ref[0:1, :], F32(1.0), F32(0.0)) - jnp.where(
        station == pair_ref[1:2, :], F32(1.0), F32(0.0)
    )
    uv_ref[...] = jnp.dot(coord_rows[...].astype(BF16), pick.astype(BF16), preferred_element_type=F32)
    uv = uv_ref[0:2, :] + uv_ref[2:4, :] + uv_ref[4:6, :]
    uv_ref[0:2, :] = uv
    uv_ref[2:8, :] = jnp.zeros((6, base_dev), F32)
    geo = lax.dot_general(
        lmp[:, 0:dpad], uv_ref[0:8, :], TN, precision=HIGHEST, preferred_element_type=F32
    )
    for j in range(tiles):
        v = vis_tile(j)
        gram = lax.dot_general(v, v, TN, preferred_element_type=F32)
        g1, g2, g3 = split3(gram)
        gsplit[j, 0] = g1.astype(BF16)
        gsplit[j, 1] = g2.astype(BF16)
        gsplit[j, 2] = g3.astype(BF16)
    opening = (my_chan * chan_dev).astype(F32) * F32(PHASE_SCALE / channels) + F32(PHASE_SCALE)
    for j in range(tiles):
        part = geo[:, j * tile : (j + 1) * tile]
        cos, sin = sincos(opening * part)
        cos_step, sin_step = sincos(F32(PHASE_SCALE / channels) * part)
        for c in range(chan_dev):
            if c:
                cos, sin = cos * cos_step - sin * sin_step, sin * cos_step + cos * sin_step
            resp[j, :, c * tile : (c + 1) * tile] = cos.astype(BF16)
            resp[j, :, (chan_dev + c) * tile : (chan_dev + c + 1) * tile] = sin.astype(BF16)

    member_rows = member[0:GROUP]
    halves = []
    for j in range(tiles):
        r = resp[j]
        model = lax.dot_general(r, r, NT, preferred_element_type=F32)
        halves.append(jnp.dot(member_rows, model * beam_gram, precision=HIGHEST, preferred_element_type=F32))
    nbuf[my_chan] = jnp.concatenate(halves, axis=1)
    push(nbuf, my_chan, n_chan, along_chan, SUB_ITERS)

    def advance(block, step):
        parts = []
        for j in range(tiles):
            z1, z2, z3 = split3(block[j])
            lhs = jnp.concatenate([z1, z2, z3, jnp.zeros_like(z1)], axis=0).astype(BF16)
            p1 = jnp.dot(lhs, gsplit[j, 0], preferred_element_type=F32)
            p2 = jnp.dot(lhs, gsplit[j, 1], preferred_element_type=F32)
            p3 = jnp.dot(lhs, gsplit[j, 2], preferred_element_type=F32)
            low = p1[2 * rank : 3 * rank] + p2[rank : 2 * rank] + p3[:rank]
            parts.append(p1[:rank] + (p1[rank : 2 * rank] + p2[:rank] + low))
        ybuf[step, my_chan] = jnp.concatenate(parts, axis=0)
        push(ybuf.at[step], my_chan, n_chan, along_chan, step)

    def gathered(step):
        arrived(ybuf.at[step], n_chan, step)
        return orthonormal(total(ybuf.at[step], n_chan).reshape(tiles, rank, times))

    advance(gathered(0), 1)

    weighted = []
    for j in range(tiles):
        at = slice(j * dpad, (j + 1) * dpad)
        bp = jnp.dot(resp[j], vis_tile(j), preferred_element_type=F32)
        weighted.append(bp * tb)
        for ref, part in ((bsplit, bp), (tsplit, tb)):
            b1, b2, b3 = split3(part)
            ref[0, at] = b1.astype(BF16)
            ref[1, at] = b2.astype(BF16)
            ref[2, at] = b3.astype(BF16)

    arrived(nbuf, n_chan, SUB_ITERS)
    sub = lax.broadcasted_iota(jnp.int32, (GROUP, LANES), 0)
    lane = lax.broadcasted_iota(jnp.int32, (GROUP, LANES), 1)
    eye = jnp.where(sub == lane, F32(1.0), F32(0.0))
    n1, n2, n3 = split3(total(nbuf, n_chan))
    lhs = jnp.concatenate([n1, n2, n3], axis=0).astype(BF16)
    wide = jnp.dot(lhs, spread[...], preferred_element_type=F32)
    wide = wide[:GROUP] + (wide[GROUP : 2 * GROUP] + wide[2 * GROUP :])
    cols = [wide[:, m * LANES : (m + 1) * LANES] for m in range(CL)]
    trace = cols[0][0:1]
    for m in range(1, CL):
        trace = trace + cols[m][m : m + 1]
    recip = F32(1.0) / (F32(RHO_SCALE) * trace / F32(CL))
    inv_rho = [recip[:, j * GROUP : j * GROUP + 1] for j in range(tiles)]
    cols = [jnp.where(sub == m, F32(1.0), F32(0.0)) + cols[m] * recip for m in range(CL)]
    for p in range(CL):
        col = cols[p]
        d = F32(1.0) / col[p : p + 1]
        for m in range(CL):
            if m != p:
                f = cols[m][p : p + 1] * d
                cols[m] = jnp.where(sub == p, f, cols[m] - col * f)
        cols[p] = jnp.where(sub == p, d, -col * d)
    first = jnp.zeros((GROUP, LANES), F32)
    for m in range(CL):
        here = (lax.rem(lane, GROUP) == m) & (lane < tiles * GROUP)
        first = jnp.where(here, jnp.where(sub == m, F32(1.0), F32(0.0)) - cols[m], first)

    def times_of(a, b):
        return jnp.dot(a, b, precision=HIGHEST, preferred_element_type=F32)

    def blocks(m):
        rows = [jnp.where(lax.div(lane, GROUP) == j, m, F32(0.0)) for j in range(tiles)]
        return jnp.concatenate(rows + [jnp.zeros((LANES - tiles * GROUP, LANES), F32)], axis=0)

    e1 = blocks(first)
    second = times_of(first, e1)
    e2 = blocks(second)
    third = times_of(second, e1)
    later = times_of(jnp.concatenate([second, third], axis=0), e2)
    powers = [first, second, third, later[:GROUP], later[GROUP:], times_of(later[:GROUP], e2)]
    group = lax.div(lane, GROUP)
    by_tile = []
    for j in range(tiles):
        out = jnp.zeros((GROUP, LANES), F32)
        for p in range(ADMM_ITERS):
            shift = (p - j) * GROUP % LANES
            m = pltpu.roll(powers[p], shift, 1) if shift else powers[p]
            out = jnp.where(group == p, m, out)
        by_tile.append(out)
    packed = by_tile[0]
    for j in range(1, tiles):
        packed = packed + by_tile[j]
    mbuf[my_bl] = packed
    push(mbuf, my_bl, n_bl, along_bl, SUB_ITERS + 1)
    eye_all = jnp.where(lax.rem(lane, GROUP) == sub, F32(1.0), F32(0.0))
    eye_all = jnp.where(lane < tiles * GROUP, eye_all, F32(0.0))
    powers = [eye_all] + powers

    advance(gathered(1), 2)

    before_ref[...] = lax.dot_general(
        jnp.ones((8, times), F32), jnp.concatenate(weighted, axis=0), NT, precision=HIGHEST, preferred_element_type=F32
    )
    eye_rep = jnp.where((lax.rem(lane, GROUP) == sub) & (group < ADMM_ITERS), F32(1.0), F32(0.0))
    final = powers[ADMM_ITERS - 1] - powers[ADMM_ITERS]
    for j in range(tiles):
        own = jnp.where(group == j, final, F32(0.0))
        both = jnp.concatenate([eye_rep - by_tile[j], own], axis=1) * inv_rho[j]
        q1, q2, q3 = split3(
            lax.dot_general(member_rows, both, TN, precision=HIGHEST, preferred_element_type=F32)
        )
        at = slice(j * dpad, (j + 1) * dpad)
        qsplit[0, at] = q1.astype(BF16)
        qsplit[1, at] = q2.astype(BF16)
        qsplit[2, at] = q3.astype(BF16)

    def stacked(row):
        a, b, c = split3(row)
        at = lax.broadcasted_iota(jnp.int32, (16, row.shape[1]), 0)
        return jnp.where(at == 0, a, jnp.where(at == 1, b, jnp.where(at == 2, c, F32(0.0)))).astype(BF16)

    def row_times(row, parts):
        lhs = stacked(row)
        at = lax.broadcasted_iota(jnp.int32, (16, parts[0].shape[1]), 0)
        acc = jnp.where(at < 1, jnp.dot(lhs, parts[2], preferred_element_type=F32), F32(0.0))
        acc = acc + jnp.where(at < 2, jnp.dot(lhs, parts[1], preferred_element_type=F32), F32(0.0))
        acc = acc + jnp.where(at < 3, jnp.dot(lhs, parts[0], preferred_element_type=F32), F32(0.0))
        return jnp.sum(acc, axis=0, keepdims=True)

    def along_times(lhs, ref):
        acc = lax.dot_general(lhs, ref[2], NT, preferred_element_type=F32)
        acc = acc + lax.dot_general(lhs, ref[1], NT, preferred_element_type=F32)
        return acc + lax.dot_general(lhs, ref[0], NT, preferred_element_type=F32)

    basis = gathered(2).astype(BF16).astype(F32).reshape(tiles * rank, times)
    rows16 = basis.astype(BF16)
    product = along_times(rows16, bsplit) * along_times(rows16, tsplit)
    row_tile = lax.div(lax.broadcasted_iota(jnp.int32, product.shape, 0), rank)
    lane_tile = lax.div(lax.broadcasted_iota(jnp.int32, product.shape, 1), dpad)
    product = jnp.where(row_tile == lane_tile, product, F32(0.0))
    rhs_row = before_ref[0:1] - jnp.sum(product, axis=0, keepdims=True)
    row = row_times(rhs_row, (qsplit[0], qsplit[1], qsplit[2]))
    vbuf[my_id] = row[:, 0:LANES]
    lbuf[my_chan] = row[:, LANES : 2 * LANES]
    push(vbuf, my_id, n_all, everyone, SUB_ITERS + 2)
    push(lbuf, my_chan, n_chan, along_chan, SUB_ITERS + 3)

    part_lane = lax.broadcasted_iota(jnp.int32, (1, 4 * rank), 1)
    for j in range(tiles):
        own = basis[j * rank : (j + 1) * rank]
        wide = jnp.concatenate([own, own, own, jnp.zeros_like(own)], axis=0).astype(BF16)
        v = vis_tile(j)
        proj = lax.dot_general(v, wide, NT, preferred_element_type=F32)
        a, b, c = split3(proj)
        parts = jnp.where(part_lane < rank, a, jnp.where(part_lane < 2 * rank, b, c)).astype(BF16)
        correction = jnp.dot(parts, wide, preferred_element_type=F32)
        clean_ref[:, :, j * tile : (j + 1) * tile, :] = (
            (v.astype(F32) - correction).astype(BF16).reshape(2, chan_dev, tile, times)
        )

    arrived(mbuf, n_bl, SUB_ITERS + 1)
    moments = jnp.where(group < ADMM_ITERS - 1, total(mbuf, n_bl) * F32(1.0 / tiles_all), F32(0.0))
    history = jnp.where(group == 0, eye, pltpu.roll(moments, GROUP, 1))
    gain = jnp.where(group < ADMM_ITERS - 1, history, F32(0.0)) - F32(2.0) * moments
    local = []
    for i in range(1, ADMM_ITERS - 1):
        k = ADMM_ITERS - 2 - i
        local.append(F32(3.0) * powers[k + 1] - powers[k] - F32(2.0) * powers[k + 2])
    local.append(F32(2.0) * (powers[0] - powers[1]))
    apply = [jnp.where(lane == sub + tiles * GROUP, F32(1.0), F32(0.0))]
    for k in range(ADMM_ITERS - 2, -1, -1):
        pad = jnp.zeros((LANES - len(apply) * GROUP, LANES), F32)
        apply.insert(0, local[k] + times_of(gain, jnp.concatenate(apply + [pad], axis=0)))
    factor = F32((channels * tile * times) ** 0.5)
    pad = jnp.zeros((LANES - len(apply) * GROUP, LANES), F32)
    apply = jnp.concatenate(apply + [pad], axis=0) * F32((channels * tile * times) ** 0.5 / tiles_all)
    parts = tuple(part.astype(BF16) for part in split3(apply))
    arrived(vbuf, n_all, SUB_ITERS + 2)
    arrived(lbuf, n_chan, SUB_ITERS + 3)
    x = row_times(total(vbuf, n_all), parts) + total(lbuf, n_chan) * factor
    x = jnp.broadcast_to(x, (8, LANES))
    for j in range(tiles):
        at = x if j == 0 else pltpu.roll(x, LANES - j * GROUP, 1)
        gains_ref[j : j + 1, :] = at[0:1, 0:CL]
    cons_ref[...] = pltpu.roll(x, LANES - tiles * GROUP, 1)[0:1, 0:CL]

    for step in range(SUB_ITERS):
        sent(ybuf.at[step], n_chan, step)
    sent(nbuf, n_chan, SUB_ITERS)
    sent(mbuf, n_bl, SUB_ITERS + 1)
    sent(vbuf, n_all, SUB_ITERS + 2)
    sent(lbuf, n_chan, SUB_ITERS + 3)


def store_kernel(clean_in, gains_in, cons_in, clean_out, gains_out, cons_out, sems):
    parts, chans = clean_in.shape[:2]
    stores = [
        pltpu.make_async_copy(gains_in, gains_out, sems.at[0]),
        pltpu.make_async_copy(cons_in, cons_out, sems.at[1]),
    ]
    for p in range(parts):
        for c in range(chans):
            stores.append(
                pltpu.make_async_copy(clean_in.at[p, c], clean_out.at[p, c], sems.at[2 + p * chans + c])
            )
    for store in stores:
        store.start()
    for store in stores:
        store.wait()


def per_device(vis, station_pair_index, station_coords, dir_lm, time_beam, dir_cluster, seed_block):
    n_chan = lax.axis_size("chan")
    n_bl = lax.axis_size("bl")
    chan_dev, base_dev, times = vis.shape[1:]
    tiles, _, rank = seed_block.shape
    tile = base_dev // tiles
    dirs = dir_lm.shape[0]
    dpad = (dirs + 15) // 16 * 16
    stations = station_coords.shape[0]
    vmem = pl.BlockSpec(memory_space=pltpu.VMEM)
    anywhere = pl.BlockSpec(memory_space=pl.ANY)
    shapes = (
        jax.ShapeDtypeStruct(vis.shape, BF16),
        jax.ShapeDtypeStruct((tiles, CL), F32),
        jax.ShapeDtypeStruct((1, CL), F32),
    )
    results = pl.pallas_call(
        functools.partial(main_kernel, n_chan, n_bl, chan_dev * n_chan),
        out_shape=tuple(pltpu.VMEM(s.shape, s.dtype) for s in shapes),
        in_specs=[anywhere] * 7,
        out_specs=(vmem, vmem, vmem),
        scratch_shapes=[
            pltpu.VMEM(vis.shape, BF16),
            pltpu.VMEM((2, base_dev), jnp.int32),
            pltpu.VMEM((2, stations), F32),
            pltpu.VMEM((2, dirs), F32),
            pltpu.VMEM((dirs, times), F32),
            pltpu.VMEM((1, dirs), jnp.int32),
            pltpu.VMEM((tiles, rank, times), jnp.int32),
            pltpu.VMEM((tiles, 3, times, times), BF16),
            pltpu.VMEM((tiles, dpad, 2 * chan_dev * tile), BF16),
            pltpu.VMEM((8, LANES), F32),
            pltpu.VMEM((dpad, times), F32),
            pltpu.VMEM((8, LANES), jnp.int32),
            pltpu.VMEM((GROUP, stations), F32),
            pltpu.VMEM((GROUP, base_dev), F32),
            pltpu.VMEM((3, tiles * dpad, times), BF16),
            pltpu.VMEM((3, tiles * dpad, times), BF16),
            pltpu.VMEM((3, tiles * dpad, 2 * LANES), BF16),
            pltpu.VMEM((8, tiles * dpad), F32),
            pltpu.VMEM((tiles * dpad, CL * LANES), BF16),
            pltpu.VMEM((SUB_ITERS, n_chan, tiles * rank, times), F32),
            pltpu.VMEM((n_chan, GROUP, tiles * dpad), F32),
            pltpu.VMEM((n_bl, GROUP, LANES), F32),
            pltpu.VMEM((n_chan * n_bl, 1, LANES), F32),
            pltpu.VMEM((n_chan, 1, LANES), F32),
            pltpu.SemaphoreType.DMA((SUB_ITERS + 4,)),
            pltpu.SemaphoreType.DMA((SUB_ITERS + 4,)),
            pltpu.SemaphoreType.DMA((tiles,)),
            pltpu.SemaphoreType.DMA((6,)),
        ],
        compiler_params=pltpu.CompilerParams(
            collective_id=0, has_side_effects=True, vmem_limit_bytes=32 * 1024 * 1024
        ),
    )(
        *(
            pltpu.with_memory_space_constraint(a, pltpu.HBM)
            for a in (
                vis,
                station_pair_index.T,
                station_coords.T,
                dir_lm.T,
                time_beam,
                dir_cluster.reshape(1, dirs),
                jnp.swapaxes(seed_block, 1, 2),
            )
        )
    )
    clean, gains, consensus = pl.pallas_call(
        store_kernel,
        out_shape=shapes,
        in_specs=[vmem] * 3,
        out_specs=(anywhere, anywhere, anywhere),
        scratch_shapes=[pltpu.SemaphoreType.DMA((2 + 2 * chan_dev,))],
        compiler_params=pltpu.CompilerParams(vmem_limit_bytes=8 * 1024 * 1024),
    )(*results)
    return clean, gains, consensus.reshape(CL)


def solution(mesh):
    placed = (P(None, "chan", "bl", None), P("bl", None), P(), P(), P(), P(), P("bl", None, None))
    return jax.shard_map(
        per_device,
        mesh=mesh,
        in_specs=placed,
        out_specs=(P(None, "chan", "bl", None), P("bl", None), P()),
        check_vma=False,
    )
```

```python
import functools

import jax
import jax.numpy as jnp
from jax import lax
from jax.experimental import pallas as pl
from jax.experimental.pallas import tpu as pltpu
from jax.sharding import PartitionSpec as P

CL = 12
SUB_ITERS = 3
ADMM_ITERS = 6
PHASE_SCALE = 20.0
RHO_SCALE = 0.5

HIGHEST = lax.Precision.HIGHEST
MESH = pl.DeviceIdType.MESH
F32 = jnp.float32
BF16 = jnp.bfloat16
LANES = 128
GROUP = 16
NT = (((1,), (1,)), ((), ()))
TN = (((0,), (0,)), ((), ()))


def split3(x):
    a = x.astype(BF16).astype(F32)
    rest = x - a
    b = rest.astype(BF16).astype(F32)
    return a, b, rest - b


def sincos(phase):
    k = jnp.floor(phase * F32(0.6366197723675814) + F32(0.5))
    r = phase - k * F32(1.5703125)
    r = r - k * F32(4.837512969970703125e-4)
    r = r - k * F32(7.54978995489188216e-8)
    r2 = r * r
    s = r + r * r2 * (F32(-1.6666654611e-1) + r2 * (F32(8.3321608736e-3) + r2 * F32(-1.9515295891e-4)))
    c = (F32(1.0) - F32(0.5) * r2) + r2 * r2 * (
        F32(4.166664568298827e-2) + r2 * (F32(-1.388731625493765e-3) + r2 * F32(2.443315711809948e-5))
    )
    ki = k.astype(jnp.int32)
    odd = (ki & 1) == 1
    cos = jnp.where(odd, s, c)
    sin = jnp.where(odd, c, s)
    cos = jnp.where(((ki + 1) & 2) == 2, -cos, cos)
    sin = jnp.where((ki & 2) == 2, -sin, sin)
    return cos, sin


def orthonormal(rows):
    count = rows.shape[1]
    sub = lax.broadcasted_iota(jnp.int32, (1, count, 1), 1)
    cols = [jnp.sum(rows * rows[:, k : k + 1, :], axis=-1, keepdims=True) for k in range(count)]
    square = cols[0][:, 0:1, :]
    for k in range(count):
        pivot = cols[k][:, k : k + 1, :]
        square = jnp.where(sub == k, pivot, square)
        if k == count - 1:
            break
        ratio = jnp.where(sub > k, cols[k] * (F32(1.0) / pivot), F32(0.0))
        for m in range(k + 1, count):
            cols[m] = cols[m] - ratio * cols[m][:, k : k + 1, :]
        rows = rows - ratio * rows[:, k : k + 1, :]
    return rows * lax.rsqrt(square)


def main_kernel(
    n_chan, n_bl, channels,
    vis_hbm, pair_hbm, coords_hbm, lm_hbm, tb_hbm, cluster_hbm, seed_hbm,
    clean_ref, gains_ref, cons_ref,
    vis_ref, pair_ref, coords_ref, lm_ref, tb_ref, cluster_ref, seed_ref,
    gsplit, resp, lmp, tbp, clp, coord_rows, uv_ref, bsplit, tsplit, qsplit, before_ref, spread,
    ybuf, nbuf, mbuf, vbuf, lbuf, send_sems, recv_sems, vis_sems, load_sems,
):
    chan_dev, base_dev, times = vis_ref.shape[1:]
    tiles, rank = seed_ref.shape[0], seed_ref.shape[1]
    tile = base_dev // tiles
    dirs = tb_ref.shape[0]
    dpad = tbp.shape[0]
    stations = coords_ref.shape[1]
    n_all = n_chan * n_bl
    tiles_all = tiles * n_bl
    my_chan = lax.axis_index("chan")
    my_bl = lax.axis_index("bl")
    my_id = my_chan * n_bl + my_bl

    loads = [
        pltpu.make_async_copy(src, dst, load_sems.at[i])
        for i, (src, dst) in enumerate(
            (
                (seed_hbm, seed_ref),
                (pair_hbm, pair_ref),
                (coords_hbm, coords_ref),
                (lm_hbm, lm_ref),
                (tb_hbm, tb_ref),
                (cluster_hbm, cluster_ref),
            )
        )
    ]
    vis_loads = []
    for j in range(tiles):
        at = (slice(None), slice(None), pl.ds(j * tile, tile), slice(None))
        vis_loads.append(pltpu.make_async_copy(vis_hbm.at[at], vis_ref.at[at], vis_sems.at[j]))
    loads[0].start()
    for load in vis_loads:
        load.start()
    for load in loads[1:]:
        load.start()

    def everyone(off):
        other = lax.rem(my_id + off, n_all)
        return (lax.div(other, n_bl), lax.rem(other, n_bl))

    def along_chan(off):
        return (lax.rem(my_chan + off, n_chan), my_bl)

    def along_bl(off):
        return (my_chan, lax.rem(my_bl + off, n_bl))

    barrier = pltpu.get_barrier_semaphore()

    @pl.loop(1, n_all)
    def _(off):
        pl.semaphore_signal(barrier, inc=1, device_id=everyone(off), device_id_type=MESH)

    def push(buf, me, n, peer, phase):
        @pl.loop(1, n)
        def _(off):
            pltpu.make_async_remote_copy(
                src_ref=buf.at[me],
                dst_ref=buf.at[me],
                send_sem=send_sems.at[phase],
                recv_sem=recv_sems.at[phase],
                device_id=peer(off),
                device_id_type=MESH,
            ).start()

    def push_rows(step, j):
        @pl.loop(1, n_chan)
        def _(off):
            part = ybuf.at[step, my_chan, pl.ds(j * rank, rank)]
            pltpu.make_async_remote_copy(
                src_ref=part,
                dst_ref=part,
                send_sem=send_sems.at[step],
                recv_sem=recv_sems.at[step],
                device_id=along_chan(off),
                device_id_type=MESH,
            ).start()

    def arrived(buf, n, phase):
        part = buf.at[pl.ds(0, n - 1)]
        pltpu.make_async_copy(part, part, recv_sems.at[phase]).wait()

    def sent(buf, n, phase):
        part = buf.at[pl.ds(0, n - 1)]
        pltpu.make_async_copy(part, part, send_sems.at[phase]).wait()

    def total(buf, n):
        out = buf[0]
        for i in range(1, n):
            out = out + buf[i]
        return out

    def vis_tile(j):
        return vis_ref[:, :, j * tile : (j + 1) * tile, :].reshape(2 * chan_dev * tile, times)

    def seen(j):
        seed = seed_ref[j].astype(F32)
        seed = jnp.concatenate([seed, jnp.zeros_like(seed)], axis=0).astype(BF16)
        p1, p2, p3 = split3(lax.dot_general(seed, vis_tile(j), NT, preferred_element_type=F32)[:rank])
        return jnp.concatenate([p1, p2, p3, jnp.zeros_like(p1)], axis=0).astype(BF16)

    def back(lhs, j):
        acc = jnp.dot(lhs, vis_tile(j), preferred_element_type=F32)
        ybuf[0, my_chan, j * rank : (j + 1) * rank] = acc[:rank] + (acc[rank : 2 * rank] + acc[2 * rank : 3 * rank])

    loads[0].wait()
    held = None
    for j in range(tiles):
        vis_loads[j].wait()
        lhs = seen(j)
        if j:
            back(held, j - 1)
        held = lhs
    back(held, tiles - 1)
    pl.semaphore_wait(barrier, n_all - 1)
    push(ybuf.at[0], my_chan, n_chan, along_chan, 0)

    for load in loads[1:]:
        load.wait()
    lmp[...] = jnp.zeros_like(lmp)
    lmp[0:2, 0:dirs] = lm_ref[...]
    tbp[...] = jnp.zeros_like(tbp)
    tbp[0:dirs, :] = tb_ref[...]
    clp[...] = jnp.full_like(clp, -1)
    clp[0:1, 0:dirs] = cluster_ref[...]
    c1, c2, c3 = split3(coords_ref[...])
    coord_rows[...] = jnp.zeros_like(coord_rows)
    coord_rows[0:2, :] = c1
    coord_rows[2:4, :] = c2
    coord_rows[4:6, :] = c3
    tb = tbp[...]
    beam_gram = lax.dot_general(tb, tb, NT, precision=HIGHEST, preferred_element_type=F32)
    member = jnp.where(
        lax.broadcasted_iota(jnp.int32, (LANES, dpad), 0) == clp[0:1, 0:dpad], F32(1.0), F32(0.0)
    )
    named = jnp.broadcast_to(clp[0:1, :].astype(F32), (LANES, LANES)).T[0:dpad]
    lane_group = lax.rem(lax.div(lax.broadcasted_iota(jnp.int32, (dpad, LANES), 1), GROUP), tiles)
    for m in range(CL):
        hit = jnp.where(named == F32(m), F32(1.0), F32(0.0))
        for j in range(tiles):
            spread[j * dpad : (j + 1) * dpad, m * LANES : (m + 1) * LANES] = jnp.where(
                lane_group == j, hit, F32(0.0)
            ).astype(BF16)
    station = lax.broadcasted_iota(jnp.int32, (stations, base_dev), 0)
    pick = jnp.where(station == pair_ref[0:1, :], F32(1.0), F32(0.0)) - jnp.where(
        station == pair_ref[1:2, :], F32(1.0), F32(0.0)
    )
    uv_ref[...] = jnp.dot(coord_rows[...].astype(BF16), pick.astype(BF16), preferred_element_type=F32)
    uv = uv_ref[0:2, :] + uv_ref[2:4, :] + uv_ref[4:6, :]
    uv_ref[0:2, :] = uv
    uv_ref[2:8, :] = jnp.zeros((6, base_dev), F32)
    geo = lax.dot_general(
        lmp[:, 0:dpad], uv_ref[0:8, :], TN, precision=HIGHEST, preferred_element_type=F32
    )
    for j in range(tiles):
        v = vis_tile(j)
        gram = lax.dot_general(v, v, TN, preferred_element_type=F32)
        g1, g2, g3 = split3(gram)
        gsplit[j, 0] = g1.astype(BF16)
        gsplit[j, 1] = g2.astype(BF16)
        gsplit[j, 2] = g3.astype(BF16)
    opening = (my_chan * chan_dev).astype(F32) * F32(PHASE_SCALE / channels) + F32(PHASE_SCALE)
    for j in range(tiles):
        part = geo[:, j * tile : (j + 1) * tile]
        cos, sin = sincos(opening * part)
        cos_step, sin_step = sincos(F32(PHASE_SCALE / channels) * part)
        for c in range(chan_dev):
            if c:
                cos, sin = cos * cos_step - sin * sin_step, sin * cos_step + cos * sin_step
            resp[j, :, c * tile : (c + 1) * tile] = cos.astype(BF16)
            resp[j, :, (chan_dev + c) * tile : (chan_dev + c + 1) * tile] = sin.astype(BF16)

    member_rows = member[0:GROUP]
    halves = []
    for j in range(tiles):
        r = resp[j]
        model = lax.dot_general(r, r, NT, preferred_element_type=F32)
        halves.append(jnp.dot(member_rows, model * beam_gram, precision=HIGHEST, preferred_element_type=F32))
    nbuf[my_chan] = jnp.concatenate(halves, axis=1)
    push(nbuf, my_chan, n_chan, along_chan, SUB_ITERS)

    def advance(block, step):
        for j in range(tiles):
            z1, z2, z3 = split3(block[j])
            lhs = jnp.concatenate([z1, z2, z3, jnp.zeros_like(z1)], axis=0).astype(BF16)
            p1 = jnp.dot(lhs, gsplit[j, 0], preferred_element_type=F32)
            p2 = jnp.dot(lhs, gsplit[j, 1], preferred_element_type=F32)
            p3 = jnp.dot(lhs, gsplit[j, 2], preferred_element_type=F32)
            low = p1[2 * rank : 3 * rank] + p2[rank : 2 * rank] + p3[:rank]
            ybuf[step, my_chan, j * rank : (j + 1) * rank] = p1[:rank] + (p1[rank : 2 * rank] + p2[:rank] + low)
            push_rows(step, j)

    def gathered(step):
        arrived(ybuf.at[step], n_chan, step)
        return orthonormal(total(ybuf.at[step], n_chan).reshape(tiles, rank, times))

    advance(gathered(0), 1)

    weighted = []
    for j in range(tiles):
        at = slice(j * dpad, (j + 1) * dpad)
        bp = jnp.dot(resp[j], vis_tile(j), preferred_element_type=F32)
        weighted.append(bp * tb)
        for ref, part in ((bsplit, bp), (tsplit, tb)):
            b1, b2, b3 = split3(part)
            ref[0, at] = b1.astype(BF16)
            ref[1, at] = b2.astype(BF16)
            ref[2, at] = b3.astype(BF16)

    arrived(nbuf, n_chan, SUB_ITERS)
    sub = lax.broadcasted_iota(jnp.int32, (GROUP, LANES), 0)
    lane = lax.broadcasted_iota(jnp.int32, (GROUP, LANES), 1)
    eye = jnp.where(sub == lane, F32(1.0), F32(0.0))
    n1, n2, n3 = split3(total(nbuf, n_chan))
    lhs = jnp.concatenate([n1, n2, n3], axis=0).astype(BF16)
    wide = jnp.dot(lhs, spread[...], preferred_element_type=F32)
    wide = wide[:GROUP] + (wide[GROUP : 2 * GROUP] + wide[2 * GROUP :])
    cols = [wide[:, m * LANES : (m + 1) * LANES] for m in range(CL)]
    trace = cols[0][0:1]
    for m in range(1, CL):
        trace = trace + cols[m][m : m + 1]
    recip = F32(1.0) / (F32(RHO_SCALE) * trace / F32(CL))
    inv_rho = [recip[:, j * GROUP : j * GROUP + 1] for j in range(tiles)]
    cols = [jnp.where(sub == m, F32(1.0), F32(0.0)) + cols[m] * recip for m in range(CL)]
    for p in range(CL):
        col = cols[p]
        d = F32(1.0) / col[p : p + 1]
        for m in range(CL):
            if m != p:
                f = cols[m][p : p + 1] * d
                cols[m] = jnp.where(sub == p, f, cols[m] - col * f)
        cols[p] = jnp.where(sub == p, d, -col * d)
    first = jnp.zeros((GROUP, LANES), F32)
    for m in range(CL):
        here = (lax.rem(lane, GROUP) == m) & (lane < tiles * GROUP)
        first = jnp.where(here, jnp.where(sub == m, F32(1.0), F32(0.0)) - cols[m], first)

    def times_of(a, b):
        return jnp.dot(a, b, precision=HIGHEST, preferred_element_type=F32)

    def blocks(m):
        rows = [jnp.where(lax.div(lane, GROUP) == j, m, F32(0.0)) for j in range(tiles)]
        return jnp.concatenate(rows + [jnp.zeros((LANES - tiles * GROUP, LANES), F32)], axis=0)

    advance(gathered(1), 2)

    e1 = blocks(first)
    second = times_of(first, e1)
    e2 = blocks(second)
    third = times_of(second, e1)
    later = times_of(jnp.concatenate([second, third], axis=0), e2)
    powers = [first, second, third, later[:GROUP], later[GROUP:], times_of(later[:GROUP], e2)]
    group = lax.div(lane, GROUP)
    by_tile = []
    for j in range(tiles):
        out = jnp.zeros((GROUP, LANES), F32)
        for p in range(ADMM_ITERS):
            shift = (p - j) * GROUP % LANES
            m = pltpu.roll(powers[p], shift, 1) if shift else powers[p]
            out = jnp.where(group == p, m, out)
        by_tile.append(out)
    packed = by_tile[0]
    for j in range(1, tiles):
        packed = packed + by_tile[j]
    mbuf[my_bl] = packed
    push(mbuf, my_bl, n_bl, along_bl, SUB_ITERS + 1)
    eye_all = jnp.where(lax.rem(lane, GROUP) == sub, F32(1.0), F32(0.0))
    eye_all = jnp.where(lane < tiles * GROUP, eye_all, F32(0.0))
    powers = [eye_all] + powers

    before_ref[...] = lax.dot_general(
        jnp.ones((8, times), F32), jnp.concatenate(weighted, axis=0), NT, precision=HIGHEST, preferred_element_type=F32
    )
    eye_rep = jnp.where((lax.rem(lane, GROUP) == sub) & (group < ADMM_ITERS), F32(1.0), F32(0.0))
    final = powers[ADMM_ITERS - 1] - powers[ADMM_ITERS]
    for j in range(tiles):
        own = jnp.where(group == j, final, F32(0.0))
        both = jnp.concatenate([eye_rep - by_tile[j], own], axis=1) * inv_rho[j]
        q1, q2, q3 = split3(
            lax.dot_general(member_rows, both, TN, precision=HIGHEST, preferred_element_type=F32)
        )
        at = slice(j * dpad, (j + 1) * dpad)
        qsplit[0, at] = q1.astype(BF16)
        qsplit[1, at] = q2.astype(BF16)
        qsplit[2, at] = q3.astype(BF16)

    def stacked(row):
        a, b, c = split3(row)
        at = lax.broadcasted_iota(jnp.int32, (16, row.shape[1]), 0)
        return jnp.where(at == 0, a, jnp.where(at == 1, b, jnp.where(at == 2, c, F32(0.0)))).astype(BF16)

    def row_times(row, parts):
        lhs = stacked(row)
        at = lax.broadcasted_iota(jnp.int32, (16, parts[0].shape[1]), 0)
        acc = jnp.where(at < 1, jnp.dot(lhs, parts[2], preferred_element_type=F32), F32(0.0))
        acc = acc + jnp.where(at < 2, jnp.dot(lhs, parts[1], preferred_element_type=F32), F32(0.0))
        acc = acc + jnp.where(at < 3, jnp.dot(lhs, parts[0], preferred_element_type=F32), F32(0.0))
        return jnp.sum(acc, axis=0, keepdims=True)

    def along_times(lhs, ref):
        acc = lax.dot_general(lhs, ref[2], NT, preferred_element_type=F32)
        acc = acc + lax.dot_general(lhs, ref[1], NT, preferred_element_type=F32)
        return acc + lax.dot_general(lhs, ref[0], NT, preferred_element_type=F32)

    basis = gathered(2).astype(BF16).astype(F32).reshape(tiles * rank, times)
    rows16 = basis.astype(BF16)
    product = along_times(rows16, bsplit) * along_times(rows16, tsplit)
    row_tile = lax.div(lax.broadcasted_iota(jnp.int32, product.shape, 0), rank)
    lane_tile = lax.div(lax.broadcasted_iota(jnp.int32, product.shape, 1), dpad)
    product = jnp.where(row_tile == lane_tile, product, F32(0.0))
    rhs_row = before_ref[0:1] - jnp.sum(product, axis=0, keepdims=True)
    row = row_times(rhs_row, (qsplit[0], qsplit[1], qsplit[2]))
    vbuf[my_id] = row[:, 0:LANES]
    lbuf[my_chan] = row[:, LANES : 2 * LANES]
    push(vbuf, my_id, n_all, everyone, SUB_ITERS + 2)
    push(lbuf, my_chan, n_chan, along_chan, SUB_ITERS + 3)

    part_lane = lax.broadcasted_iota(jnp.int32, (1, 4 * rank), 1)
    for j in range(tiles):
        own = basis[j * rank : (j + 1) * rank]
        wide = jnp.concatenate([own, own, own, jnp.zeros_like(own)], axis=0).astype(BF16)
        v = vis_tile(j)
        proj = lax.dot_general(v, wide, NT, preferred_element_type=F32)
        a, b, c = split3(proj)
        parts = jnp.where(part_lane < rank, a, jnp.where(part_lane < 2 * rank, b, c)).astype(BF16)
        correction = jnp.dot(parts, wide, preferred_element_type=F32)
        clean_ref[:, :, j * tile : (j + 1) * tile, :] = (
            (v.astype(F32) - correction).astype(BF16).reshape(2, chan_dev, tile, times)
        )

    arrived(mbuf, n_bl, SUB_ITERS + 1)
    moments = jnp.where(group < ADMM_ITERS - 1, total(mbuf, n_bl) * F32(1.0 / tiles_all), F32(0.0))
    history = jnp.where(group == 0, eye, pltpu.roll(moments, GROUP, 1))
    gain = jnp.where(group < ADMM_ITERS - 1, history, F32(0.0)) - F32(2.0) * moments
    local = []
    for i in range(1, ADMM_ITERS - 1):
        k = ADMM_ITERS - 2 - i
        local.append(F32(3.0) * powers[k + 1] - powers[k] - F32(2.0) * powers[k + 2])
    local.append(F32(2.0) * (powers[0] - powers[1]))
    apply = [jnp.where(lane == sub + tiles * GROUP, F32(1.0), F32(0.0))]
    for k in range(ADMM_ITERS - 2, -1, -1):
        pad = jnp.zeros((LANES - len(apply) * GROUP, LANES), F32)
        apply.insert(0, local[k] + times_of(gain, jnp.concatenate(apply + [pad], axis=0)))
    factor = F32((channels * tile * times) ** 0.5)
    pad = jnp.zeros((LANES - len(apply) * GROUP, LANES), F32)
    apply = jnp.concatenate(apply + [pad], axis=0) * F32((channels * tile * times) ** 0.5 / tiles_all)
    parts = tuple(part.astype(BF16) for part in split3(apply))
    arrived(vbuf, n_all, SUB_ITERS + 2)
    arrived(lbuf, n_chan, SUB_ITERS + 3)
    x = row_times(total(vbuf, n_all), parts) + total(lbuf, n_chan) * factor
    x = jnp.broadcast_to(x, (8, LANES))
    for j in range(tiles):
        at = x if j == 0 else pltpu.roll(x, LANES - j * GROUP, 1)
        gains_ref[j : j + 1, :] = at[0:1, 0:CL]
    cons_ref[...] = pltpu.roll(x, LANES - tiles * GROUP, 1)[0:1, 0:CL]

    for step in range(SUB_ITERS):
        sent(ybuf.at[step], n_chan, step)
    sent(nbuf, n_chan, SUB_ITERS)
    sent(mbuf, n_bl, SUB_ITERS + 1)
    sent(vbuf, n_all, SUB_ITERS + 2)
    sent(lbuf, n_chan, SUB_ITERS + 3)


def store_kernel(clean_in, gains_in, cons_in, clean_out, gains_out, cons_out, sems):
    parts, chans = clean_in.shape[:2]
    stores = [
        pltpu.make_async_copy(gains_in, gains_out, sems.at[0]),
        pltpu.make_async_copy(cons_in, cons_out, sems.at[1]),
    ]
    for p in range(parts):
        for c in range(chans):
            stores.append(
                pltpu.make_async_copy(clean_in.at[p, c], clean_out.at[p, c], sems.at[2 + p * chans + c])
            )
    for store in stores:
        store.start()
    for store in stores:
        store.wait()


def per_device(vis, station_pair_index, station_coords, dir_lm, time_beam, dir_cluster, seed_block):
    n_chan = lax.axis_size("chan")
    n_bl = lax.axis_size("bl")
    chan_dev, base_dev, times = vis.shape[1:]
    tiles, _, rank = seed_block.shape
    tile = base_dev // tiles
    dirs = dir_lm.shape[0]
    dpad = (dirs + 15) // 16 * 16
    stations = station_coords.shape[0]
    vmem = pl.BlockSpec(memory_space=pltpu.VMEM)
    anywhere = pl.BlockSpec(memory_space=pl.ANY)
    shapes = (
        jax.ShapeDtypeStruct(vis.shape, BF16),
        jax.ShapeDtypeStruct((tiles, CL), F32),
        jax.ShapeDtypeStruct((1, CL), F32),
    )
    results = pl.pallas_call(
        functools.partial(main_kernel, n_chan, n_bl, chan_dev * n_chan),
        out_shape=tuple(pltpu.VMEM(s.shape, s.dtype) for s in shapes),
        in_specs=[anywhere] * 7,
        out_specs=(vmem, vmem, vmem),
        scratch_shapes=[
            pltpu.VMEM(vis.shape, BF16),
            pltpu.VMEM((2, base_dev), jnp.int32),
            pltpu.VMEM((2, stations), F32),
            pltpu.VMEM((2, dirs), F32),
            pltpu.VMEM((dirs, times), F32),
            pltpu.VMEM((1, dirs), jnp.int32),
            pltpu.VMEM((tiles, rank, times), jnp.int32),
            pltpu.VMEM((tiles, 3, times, times), BF16),
            pltpu.VMEM((tiles, dpad, 2 * chan_dev * tile), BF16),
            pltpu.VMEM((8, LANES), F32),
            pltpu.VMEM((dpad, times), F32),
            pltpu.VMEM((8, LANES), jnp.int32),
            pltpu.VMEM((GROUP, stations), F32),
            pltpu.VMEM((GROUP, base_dev), F32),
            pltpu.VMEM((3, tiles * dpad, times), BF16),
            pltpu.VMEM((3, tiles * dpad, times), BF16),
            pltpu.VMEM((3, tiles * dpad, 2 * LANES), BF16),
            pltpu.VMEM((8, tiles * dpad), F32),
            pltpu.VMEM((tiles * dpad, CL * LANES), BF16),
            pltpu.VMEM((SUB_ITERS, n_chan, tiles * rank, times), F32),
            pltpu.VMEM((n_chan, GROUP, tiles * dpad), F32),
            pltpu.VMEM((n_bl, GROUP, LANES), F32),
            pltpu.VMEM((n_chan * n_bl, 1, LANES), F32),
            pltpu.VMEM((n_chan, 1, LANES), F32),
            pltpu.SemaphoreType.DMA((SUB_ITERS + 4,)),
            pltpu.SemaphoreType.DMA((SUB_ITERS + 4,)),
            pltpu.SemaphoreType.DMA((tiles,)),
            pltpu.SemaphoreType.DMA((6,)),
        ],
        compiler_params=pltpu.CompilerParams(
            collective_id=0, has_side_effects=True, vmem_limit_bytes=32 * 1024 * 1024
        ),
    )(
        *(
            pltpu.with_memory_space_constraint(a, pltpu.HBM)
            for a in (
                vis,
                station_pair_index.T,
                station_coords.T,
                dir_lm.T,
                time_beam,
                dir_cluster.reshape(1, dirs),
                jnp.swapaxes(seed_block, 1, 2),
            )
        )
    )
    clean, gains, consensus = pl.pallas_call(
        store_kernel,
        out_shape=shapes,
        in_specs=[vmem] * 3,
        out_specs=(anywhere, anywhere, anywhere),
        scratch_shapes=[pltpu.SemaphoreType.DMA((2 + 2 * chan_dev,))],
        compiler_params=pltpu.CompilerParams(vmem_limit_bytes=8 * 1024 * 1024),
    )(*results)
    return clean, gains, consensus.reshape(CL)


def solution(mesh):
    placed = (P(None, "chan", "bl", None), P("bl", None), P(), P(), P(), P(), P("bl", None, None))
    return jax.shard_map(
        per_device,
        mesh=mesh,
        in_specs=placed,
        out_specs=(P(None, "chan", "bl", None), P("bl", None), P()),
        check_vma=False,
    )
```

```python
import functools

import jax
import jax.numpy as jnp
from jax import lax
from jax.experimental import pallas as pl
from jax.experimental.pallas import tpu as pltpu
from jax.sharding import PartitionSpec as P

CL = 12
SUB_ITERS = 3
ADMM_ITERS = 6
PHASE_SCALE = 20.0
RHO_SCALE = 0.5

HIGHEST = lax.Precision.HIGHEST
MESH = pl.DeviceIdType.MESH
F32 = jnp.float32
BF16 = jnp.bfloat16
LANES = 128
GROUP = 16
GATE = 4
NT = (((1,), (1,)), ((), ()))
TN = (((0,), (0,)), ((), ()))


def split3(x):
    a = x.astype(BF16).astype(F32)
    rest = x - a
    b = rest.astype(BF16).astype(F32)
    return a, b, rest - b


def sincos(phase):
    k = jnp.floor(phase * F32(0.6366197723675814) + F32(0.5))
    r = phase - k * F32(1.5703125)
    r = r - k * F32(4.837512969970703125e-4)
    r = r - k * F32(7.54978995489188216e-8)
    r2 = r * r
    s = r + r * r2 * (F32(-1.6666654611e-1) + r2 * (F32(8.3321608736e-3) + r2 * F32(-1.9515295891e-4)))
    c = (F32(1.0) - F32(0.5) * r2) + r2 * r2 * (
        F32(4.166664568298827e-2) + r2 * (F32(-1.388731625493765e-3) + r2 * F32(2.443315711809948e-5))
    )
    ki = k.astype(jnp.int32)
    odd = (ki & 1) == 1
    cos = jnp.where(odd, s, c)
    sin = jnp.where(odd, c, s)
    cos = jnp.where(((ki + 1) & 2) == 2, -cos, cos)
    sin = jnp.where((ki & 2) == 2, -sin, sin)
    return cos, sin


def orthonormal(rows):
    count = rows.shape[1]
    sub = lax.broadcasted_iota(jnp.int32, (1, count, 1), 1)
    cols = [jnp.sum(rows * rows[:, k : k + 1, :], axis=-1, keepdims=True) for k in range(count)]
    square = cols[0][:, 0:1, :]
    for k in range(count):
        pivot = cols[k][:, k : k + 1, :]
        square = jnp.where(sub == k, pivot, square)
        if k == count - 1:
            break
        ratio = jnp.where(sub > k, cols[k] * (F32(1.0) / pivot), F32(0.0))
        for m in range(k + 1, count):
            cols[m] = cols[m] - ratio * cols[m][:, k : k + 1, :]
        rows = rows - ratio * rows[:, k : k + 1, :]
    return rows * lax.rsqrt(square)


def main_kernel(
    n_chan, n_bl, channels,
    vis_hbm, pair_hbm, coords_hbm, lm_hbm, tb_hbm, cluster_hbm, seed_hbm,
    clean_ref, gains_ref, cons_ref,
    vis_ref, pair_ref, coords_ref, lm_ref, tb_ref, cluster_ref, seed_ref,
    gsplit, resp, lmp, tbp, clp, coord_rows, uv_ref, bsplit, tsplit, qsplit, before_ref, spread,
    ybuf, nbuf, mbuf, vbuf, lbuf, send_sems, recv_sems, vis_sems, load_sems, all_in,
):
    chan_dev, base_dev, times = vis_ref.shape[1:]
    tiles, rank = seed_ref.shape[0], seed_ref.shape[1]
    tile = base_dev // tiles
    dirs = tb_ref.shape[0]
    dpad = tbp.shape[0]
    stations = coords_ref.shape[1]
    n_all = n_chan * n_bl
    tiles_all = tiles * n_bl
    my_chan = lax.axis_index("chan")
    my_bl = lax.axis_index("bl")
    my_id = my_chan * n_bl + my_bl

    loads = [
        pltpu.make_async_copy(src, dst, load_sems.at[i])
        for i, (src, dst) in enumerate(
            (
                (seed_hbm, seed_ref),
                (pair_hbm, pair_ref),
                (coords_hbm, coords_ref),
                (lm_hbm, lm_ref),
                (tb_hbm, tb_ref),
                (cluster_hbm, cluster_ref),
            )
        )
    ]
    vis_loads = []
    for j in range(tiles):
        at = (slice(None), slice(None), pl.ds(j * tile, tile), slice(None))
        vis_loads.append(pltpu.make_async_copy(vis_hbm.at[at], vis_ref.at[at], vis_sems.at[j]))
    loads[0].start()
    for load in vis_loads:
        load.start()
    for load in loads[1:]:
        load.start()

    def everyone(off):
        other = lax.rem(my_id + off, n_all)
        return (lax.div(other, n_bl), lax.rem(other, n_bl))

    def along_chan(off):
        return (lax.rem(my_chan + off, n_chan), my_bl)

    def along_bl(off):
        return (my_chan, lax.rem(my_bl + off, n_bl))

    barrier = pltpu.get_barrier_semaphore()

    inner = GATE if n_bl % GATE == 0 else 1
    outer = n_bl // inner
    my_outer, my_inner = lax.div(my_bl, inner), lax.rem(my_bl, inner)

    def near(off):
        other = lax.rem(my_chan * inner + my_inner + off, n_chan * inner)
        return (lax.div(other, inner), my_outer * inner + lax.rem(other, inner))

    def line(off):
        return (my_chan, lax.rem(my_outer + off, outer) * inner + my_inner)

    @pl.loop(1, n_chan * inner)
    def _(off):
        pl.semaphore_signal(barrier, inc=1, device_id=near(off), device_id_type=MESH)

    @pl.loop(1, outer)
    def _(off):
        pl.semaphore_signal(barrier, inc=1, device_id=line(off), device_id_type=MESH)

    def push(buf, me, n, peer, phase):
        @pl.loop(1, n)
        def _(off):
            pltpu.make_async_remote_copy(
                src_ref=buf.at[me],
                dst_ref=buf.at[me],
                send_sem=send_sems.at[phase],
                recv_sem=recv_sems.at[phase],
                device_id=peer(off),
                device_id_type=MESH,
            ).start()

    def push_rows(step, j):
        @pl.loop(1, n_chan)
        def _(off):
            part = ybuf.at[step, my_chan, pl.ds(j * rank, rank)]
            pltpu.make_async_remote_copy(
                src_ref=part,
                dst_ref=part,
                send_sem=send_sems.at[step],
                recv_sem=recv_sems.at[step],
                device_id=along_chan(off),
                device_id_type=MESH,
            ).start()

    def arrived(buf, n, phase):
        part = buf.at[pl.ds(0, n - 1)]
        pltpu.make_async_copy(part, part, recv_sems.at[phase]).wait()

    def sent(buf, n, phase):
        part = buf.at[pl.ds(0, n - 1)]
        pltpu.make_async_copy(part, part, send_sems.at[phase]).wait()

    def total(buf, n):
        out = buf[0]
        for i in range(1, n):
            out = out + buf[i]
        return out

    def vis_tile(j):
        return vis_ref[:, :, j * tile : (j + 1) * tile, :].reshape(2 * chan_dev * tile, times)

    def seen(j):
        seed = seed_ref[j].astype(F32)
        seed = jnp.concatenate([seed, jnp.zeros_like(seed)], axis=0).astype(BF16)
        p1, p2, p3 = split3(lax.dot_general(seed, vis_tile(j), NT, preferred_element_type=F32)[:rank])
        return jnp.concatenate([p1, p2, p3, jnp.zeros_like(p1)], axis=0).astype(BF16)

    def back(lhs, j):
        acc = jnp.dot(lhs, vis_tile(j), preferred_element_type=F32)
        ybuf[0, my_chan, j * rank : (j + 1) * rank] = acc[:rank] + (acc[rank : 2 * rank] + acc[2 * rank : 3 * rank])

    loads[0].wait()
    held = None
    for j in range(tiles):
        vis_loads[j].wait()
        lhs = seen(j)
        if j:
            back(held, j - 1)
        held = lhs
    back(held, tiles - 1)
    pl.semaphore_wait(barrier, n_chan * inner - 1 + outer - 1)
    push(ybuf.at[0], my_chan, n_chan, along_chan, 0)

    @pl.loop(1, outer)
    def _(off):
        pl.semaphore_signal(all_in, inc=1, device_id=line(off), device_id_type=MESH)

    for load in loads[1:]:
        load.wait()
    lmp[...] = jnp.zeros_like(lmp)
    lmp[0:2, 0:dirs] = lm_ref[...]
    tbp[...] = jnp.zeros_like(tbp)
    tbp[0:dirs, :] = tb_ref[...]
    clp[...] = jnp.full_like(clp, -1)
    clp[0:1, 0:dirs] = cluster_ref[...]
    c1, c2, c3 = split3(coords_ref[...])
    coord_rows[...] = jnp.zeros_like(coord_rows)
    coord_rows[0:2, :] = c1
    coord_rows[2:4, :] = c2
    coord_rows[4:6, :] = c3
    tb = tbp[...]
    beam_gram = lax.dot_general(tb, tb, NT, precision=HIGHEST, preferred_element_type=F32)
    member = jnp.where(
        lax.broadcasted_iota(jnp.int32, (LANES, dpad), 0) == clp[0:1, 0:dpad], F32(1.0), F32(0.0)
    )
    named = jnp.broadcast_to(clp[0:1, :].astype(F32), (LANES, LANES)).T[0:dpad]
    lane_group = lax.rem(lax.div(lax.broadcasted_iota(jnp.int32, (dpad, LANES), 1), GROUP), tiles)
    for m in range(CL):
        hit = jnp.where(named == F32(m), F32(1.0), F32(0.0))
        for j in range(tiles):
            spread[j * dpad : (j + 1) * dpad, m * LANES : (m + 1) * LANES] = jnp.where(
                lane_group == j, hit, F32(0.0)
            ).astype(BF16)
    station = lax.broadcasted_iota(jnp.int32, (stations, base_dev), 0)
    pick = jnp.where(station == pair_ref[0:1, :], F32(1.0), F32(0.0)) - jnp.where(
        station == pair_ref[1:2, :], F32(1.0), F32(0.0)
    )
    uv_ref[...] = jnp.dot(coord_rows[...].astype(BF16), pick.astype(BF16), preferred_element_type=F32)
    uv = uv_ref[0:2, :] + uv_ref[2:4, :] + uv_ref[4:6, :]
    uv_ref[0:2, :] = uv
    uv_ref[2:8, :] = jnp.zeros((6, base_dev), F32)
    geo = lax.dot_general(
        lmp[:, 0:dpad], uv_ref[0:8, :], TN, precision=HIGHEST, preferred_element_type=F32
    )
    for j in range(tiles):
        v = vis_tile(j)
        gram = lax.dot_general(v, v, TN, preferred_element_type=F32)
        g1, g2, g3 = split3(gram)
        gsplit[j, 0] = g1.astype(BF16)
        gsplit[j, 1] = g2.astype(BF16)
        gsplit[j, 2] = g3.astype(BF16)
    opening = (my_chan * chan_dev).astype(F32) * F32(PHASE_SCALE / channels) + F32(PHASE_SCALE)
    for j in range(tiles):
        part = geo[:, j * tile : (j + 1) * tile]
        cos, sin = sincos(opening * part)
        cos_step, sin_step = sincos(F32(PHASE_SCALE / channels) * part)
        for c in range(chan_dev):
            if c:
                cos, sin = cos * cos_step - sin * sin_step, sin * cos_step + cos * sin_step
            resp[j, :, c * tile : (c + 1) * tile] = cos.astype(BF16)
            resp[j, :, (chan_dev + c) * tile : (chan_dev + c + 1) * tile] = sin.astype(BF16)

    member_rows = member[0:GROUP]
    halves = []
    for j in range(tiles):
        r = resp[j]
        model = lax.dot_general(r, r, NT, preferred_element_type=F32)
        halves.append(jnp.dot(member_rows, model * beam_gram, precision=HIGHEST, preferred_element_type=F32))
    nbuf[my_chan] = jnp.concatenate(halves, axis=1)
    push(nbuf, my_chan, n_chan, along_chan, SUB_ITERS)

    def advance(block, step):
        for j in range(tiles):
            z1, z2, z3 = split3(block[j])
            lhs = jnp.concatenate([z1, z2, z3, jnp.zeros_like(z1)], axis=0).astype(BF16)
            p1 = jnp.dot(lhs, gsplit[j, 0], preferred_element_type=F32)
            p2 = jnp.dot(lhs, gsplit[j, 1], preferred_element_type=F32)
            p3 = jnp.dot(lhs, gsplit[j, 2], preferred_element_type=F32)
            low = p1[2 * rank : 3 * rank] + p2[rank : 2 * rank] + p3[:rank]
            ybuf[step, my_chan, j * rank : (j + 1) * rank] = p1[:rank] + (p1[rank : 2 * rank] + p2[:rank] + low)
            push_rows(step, j)

    def gathered(step):
        arrived(ybuf.at[step], n_chan, step)
        return orthonormal(total(ybuf.at[step], n_chan).reshape(tiles, rank, times))

    advance(gathered(0), 1)

    weighted = []
    for j in range(tiles):
        at = slice(j * dpad, (j + 1) * dpad)
        bp = jnp.dot(resp[j], vis_tile(j), preferred_element_type=F32)
        weighted.append(bp * tb)
        for ref, part in ((bsplit, bp), (tsplit, tb)):
            b1, b2, b3 = split3(part)
            ref[0, at] = b1.astype(BF16)
            ref[1, at] = b2.astype(BF16)
            ref[2, at] = b3.astype(BF16)

    arrived(nbuf, n_chan, SUB_ITERS)
    sub = lax.broadcasted_iota(jnp.int32, (GROUP, LANES), 0)
    lane = lax.broadcasted_iota(jnp.int32, (GROUP, LANES), 1)
    eye = jnp.where(sub == lane, F32(1.0), F32(0.0))
    n1, n2, n3 = split3(total(nbuf, n_chan))
    lhs = jnp.concatenate([n1, n2, n3], axis=0).astype(BF16)
    wide = jnp.dot(lhs, spread[...], preferred_element_type=F32)
    wide = wide[:GROUP] + (wide[GROUP : 2 * GROUP] + wide[2 * GROUP :])
    cols = [wide[:, m * LANES : (m + 1) * LANES] for m in range(CL)]
    trace = cols[0][0:1]
    for m in range(1, CL):
        trace = trace + cols[m][m : m + 1]
    recip = F32(1.0) / (F32(RHO_SCALE) * trace / F32(CL))
    inv_rho = [recip[:, j * GROUP : j * GROUP + 1] for j in range(tiles)]
    cols = [jnp.where(sub == m, F32(1.0), F32(0.0)) + cols[m] * recip for m in range(CL)]
    for p in range(CL):
        col = cols[p]
        d = F32(1.0) / col[p : p + 1]
        for m in range(CL):
            if m != p:
                f = cols[m][p : p + 1] * d
                cols[m] = jnp.where(sub == p, f, cols[m] - col * f)
        cols[p] = jnp.where(sub == p, d, -col * d)
    first = jnp.zeros((GROUP, LANES), F32)
    for m in range(CL):
        here = (lax.rem(lane, GROUP) == m) & (lane < tiles * GROUP)
        first = jnp.where(here, jnp.where(sub == m, F32(1.0), F32(0.0)) - cols[m], first)

    def times_of(a, b):
        return jnp.dot(a, b, precision=HIGHEST, preferred_element_type=F32)

    def blocks(m):
        rows = [jnp.where(lax.div(lane, GROUP) == j, m, F32(0.0)) for j in range(tiles)]
        return jnp.concatenate(rows + [jnp.zeros((LANES - tiles * GROUP, LANES), F32)], axis=0)

    advance(gathered(1), 2)

    e1 = blocks(first)
    second = times_of(first, e1)
    e2 = blocks(second)
    third = times_of(second, e1)
    later = times_of(jnp.concatenate([second, third], axis=0), e2)
    powers = [first, second, third, later[:GROUP], later[GROUP:], times_of(later[:GROUP], e2)]
    group = lax.div(lane, GROUP)
    by_tile = []
    for j in range(tiles):
        out = jnp.zeros((GROUP, LANES), F32)
        for p in range(ADMM_ITERS):
            shift = (p - j) * GROUP % LANES
            m = pltpu.roll(powers[p], shift, 1) if shift else powers[p]
            out = jnp.where(group == p, m, out)
        by_tile.append(out)
    packed = by_tile[0]
    for j in range(1, tiles):
        packed = packed + by_tile[j]
    mbuf[my_bl] = packed
    pl.semaphore_wait(all_in, outer - 1)
    push(mbuf, my_bl, n_bl, along_bl, SUB_ITERS + 1)
    eye_all = jnp.where(lax.rem(lane, GROUP) == sub, F32(1.0), F32(0.0))
    eye_all = jnp.where(lane < tiles * GROUP, eye_all, F32(0.0))
    powers = [eye_all] + powers

    before_ref[...] = lax.dot_general(
        jnp.ones((8, times), F32), jnp.concatenate(weighted, axis=0), NT, precision=HIGHEST, preferred_element_type=F32
    )
    eye_rep = jnp.where((lax.rem(lane, GROUP) == sub) & (group < ADMM_ITERS), F32(1.0), F32(0.0))
    final = powers[ADMM_ITERS - 1] - powers[ADMM_ITERS]
    for j in range(tiles):
        own = jnp.where(group == j, final, F32(0.0))
        both = jnp.concatenate([eye_rep - by_tile[j], own], axis=1) * inv_rho[j]
        q1, q2, q3 = split3(
            lax.dot_general(member_rows, both, TN, precision=HIGHEST, preferred_element_type=F32)
        )
        at = slice(j * dpad, (j + 1) * dpad)
        qsplit[0, at] = q1.astype(BF16)
        qsplit[1, at] = q2.astype(BF16)
        qsplit[2, at] = q3.astype(BF16)

    def stacked(row):
        a, b, c = split3(row)
        at = lax.broadcasted_iota(jnp.int32, (16, row.shape[1]), 0)
        return jnp.where(at == 0, a, jnp.where(at == 1, b, jnp.where(at == 2, c, F32(0.0)))).astype(BF16)

    def row_times(row, parts):
        lhs = stacked(row)
        at = lax.broadcasted_iota(jnp.int32, (16, parts[0].shape[1]), 0)
        acc = jnp.where(at < 1, jnp.dot(lhs, parts[2], preferred_element_type=F32), F32(0.0))
        acc = acc + jnp.where(at < 2, jnp.dot(lhs, parts[1], preferred_element_type=F32), F32(0.0))
        acc = acc + jnp.where(at < 3, jnp.dot(lhs, parts[0], preferred_element_type=F32), F32(0.0))
        return jnp.sum(acc, axis=0, keepdims=True)

    def along_times(lhs, ref):
        acc = lax.dot_general(lhs, ref[2], NT, preferred_element_type=F32)
        acc = acc + lax.dot_general(lhs, ref[1], NT, preferred_element_type=F32)
        return acc + lax.dot_general(lhs, ref[0], NT, preferred_element_type=F32)

    basis = gathered(2).astype(BF16).astype(F32).reshape(tiles * rank, times)
    rows16 = basis.astype(BF16)
    product = along_times(rows16, bsplit) * along_times(rows16, tsplit)
    row_tile = lax.div(lax.broadcasted_iota(jnp.int32, product.shape, 0), rank)
    lane_tile = lax.div(lax.broadcasted_iota(jnp.int32, product.shape, 1), dpad)
    product = jnp.where(row_tile == lane_tile, product, F32(0.0))
    rhs_row = before_ref[0:1] - jnp.sum(product, axis=0, keepdims=True)
    row = row_times(rhs_row, (qsplit[0], qsplit[1], qsplit[2]))
    vbuf[my_id] = row[:, 0:LANES]
    lbuf[my_chan] = row[:, LANES : 2 * LANES]
    push(vbuf, my_id, n_all, everyone, SUB_ITERS + 2)
    push(lbuf, my_chan, n_chan, along_chan, SUB_ITERS + 3)

    part_lane = lax.broadcasted_iota(jnp.int32, (1, 4 * rank), 1)
    for j in range(tiles):
        own = basis[j * rank : (j + 1) * rank]
        wide = jnp.concatenate([own, own, own, jnp.zeros_like(own)], axis=0).astype(BF16)
        v = vis_tile(j)
        proj = lax.dot_general(v, wide, NT, preferred_element_type=F32)
        a, b, c = split3(proj)
        parts = jnp.where(part_lane < rank, a, jnp.where(part_lane < 2 * rank, b, c)).astype(BF16)
        correction = jnp.dot(parts, wide, preferred_element_type=F32)
        clean_ref[:, :, j * tile : (j + 1) * tile, :] = (
            (v.astype(F32) - correction).astype(BF16).reshape(2, chan_dev, tile, times)
        )

    arrived(mbuf, n_bl, SUB_ITERS + 1)
    moments = jnp.where(group < ADMM_ITERS - 1, total(mbuf, n_bl) * F32(1.0 / tiles_all), F32(0.0))
    history = jnp.where(group == 0, eye, pltpu.roll(moments, GROUP, 1))
    gain = jnp.where(group < ADMM_ITERS - 1, history, F32(0.0)) - F32(2.0) * moments
    local = []
    for i in range(1, ADMM_ITERS - 1):
        k = ADMM_ITERS - 2 - i
        local.append(F32(3.0) * powers[k + 1] - powers[k] - F32(2.0) * powers[k + 2])
    local.append(F32(2.0) * (powers[0] - powers[1]))
    apply = [jnp.where(lane == sub + tiles * GROUP, F32(1.0), F32(0.0))]
    for k in range(ADMM_ITERS - 2, -1, -1):
        pad = jnp.zeros((LANES - len(apply) * GROUP, LANES), F32)
        apply.insert(0, local[k] + times_of(gain, jnp.concatenate(apply + [pad], axis=0)))
    factor = F32((channels * tile * times) ** 0.5)
    pad = jnp.zeros((LANES - len(apply) * GROUP, LANES), F32)
    apply = jnp.concatenate(apply + [pad], axis=0) * F32((channels * tile * times) ** 0.5 / tiles_all)
    parts = tuple(part.astype(BF16) for part in split3(apply))
    arrived(vbuf, n_all, SUB_ITERS + 2)
    arrived(lbuf, n_chan, SUB_ITERS + 3)
    x = row_times(total(vbuf, n_all), parts) + total(lbuf, n_chan) * factor
    x = jnp.broadcast_to(x, (8, LANES))
    for j in range(tiles):
        at = x if j == 0 else pltpu.roll(x, LANES - j * GROUP, 1)
        gains_ref[j : j + 1, :] = at[0:1, 0:CL]
    cons_ref[...] = pltpu.roll(x, LANES - tiles * GROUP, 1)[0:1, 0:CL]

    for step in range(SUB_ITERS):
        sent(ybuf.at[step], n_chan, step)
    sent(nbuf, n_chan, SUB_ITERS)
    sent(mbuf, n_bl, SUB_ITERS + 1)
    sent(vbuf, n_all, SUB_ITERS + 2)
    sent(lbuf, n_chan, SUB_ITERS + 3)


def store_kernel(clean_in, gains_in, cons_in, clean_out, gains_out, cons_out, sems):
    parts, chans = clean_in.shape[:2]
    stores = [
        pltpu.make_async_copy(gains_in, gains_out, sems.at[0]),
        pltpu.make_async_copy(cons_in, cons_out, sems.at[1]),
    ]
    for p in range(parts):
        for c in range(chans):
            stores.append(
                pltpu.make_async_copy(clean_in.at[p, c], clean_out.at[p, c], sems.at[2 + p * chans + c])
            )
    for store in stores:
        store.start()
    for store in stores:
        store.wait()


def per_device(vis, station_pair_index, station_coords, dir_lm, time_beam, dir_cluster, seed_block):
    n_chan = lax.axis_size("chan")
    n_bl = lax.axis_size("bl")
    chan_dev, base_dev, times = vis.shape[1:]
    tiles, _, rank = seed_block.shape
    tile = base_dev // tiles
    dirs = dir_lm.shape[0]
    dpad = (dirs + 15) // 16 * 16
    stations = station_coords.shape[0]
    vmem = pl.BlockSpec(memory_space=pltpu.VMEM)
    anywhere = pl.BlockSpec(memory_space=pl.ANY)
    shapes = (
        jax.ShapeDtypeStruct(vis.shape, BF16),
        jax.ShapeDtypeStruct((tiles, CL), F32),
        jax.ShapeDtypeStruct((1, CL), F32),
    )
    results = pl.pallas_call(
        functools.partial(main_kernel, n_chan, n_bl, chan_dev * n_chan),
        out_shape=tuple(pltpu.VMEM(s.shape, s.dtype) for s in shapes),
        in_specs=[anywhere] * 7,
        out_specs=(vmem, vmem, vmem),
        scratch_shapes=[
            pltpu.VMEM(vis.shape, BF16),
            pltpu.VMEM((2, base_dev), jnp.int32),
            pltpu.VMEM((2, stations), F32),
            pltpu.VMEM((2, dirs), F32),
            pltpu.VMEM((dirs, times), F32),
            pltpu.VMEM((1, dirs), jnp.int32),
            pltpu.VMEM((tiles, rank, times), jnp.int32),
            pltpu.VMEM((tiles, 3, times, times), BF16),
            pltpu.VMEM((tiles, dpad, 2 * chan_dev * tile), BF16),
            pltpu.VMEM((8, LANES), F32),
            pltpu.VMEM((dpad, times), F32),
            pltpu.VMEM((8, LANES), jnp.int32),
            pltpu.VMEM((GROUP, stations), F32),
            pltpu.VMEM((GROUP, base_dev), F32),
            pltpu.VMEM((3, tiles * dpad, times), BF16),
            pltpu.VMEM((3, tiles * dpad, times), BF16),
            pltpu.VMEM((3, tiles * dpad, 2 * LANES), BF16),
            pltpu.VMEM((8, tiles * dpad), F32),
            pltpu.VMEM((tiles * dpad, CL * LANES), BF16),
            pltpu.VMEM((SUB_ITERS, n_chan, tiles * rank, times), F32),
            pltpu.VMEM((n_chan, GROUP, tiles * dpad), F32),
            pltpu.VMEM((n_bl, GROUP, LANES), F32),
            pltpu.VMEM((n_chan * n_bl, 1, LANES), F32),
            pltpu.VMEM((n_chan, 1, LANES), F32),
            pltpu.SemaphoreType.DMA((SUB_ITERS + 4,)),
            pltpu.SemaphoreType.DMA((SUB_ITERS + 4,)),
            pltpu.SemaphoreType.DMA((tiles,)),
            pltpu.SemaphoreType.DMA((6,)),
            pltpu.SemaphoreType.REGULAR,
        ],
        compiler_params=pltpu.CompilerParams(
            collective_id=0, has_side_effects=True, vmem_limit_bytes=32 * 1024 * 1024
        ),
    )(
        *(
            pltpu.with_memory_space_constraint(a, pltpu.HBM)
            for a in (
                vis,
                station_pair_index.T,
                station_coords.T,
                dir_lm.T,
                time_beam,
                dir_cluster.reshape(1, dirs),
                jnp.swapaxes(seed_block, 1, 2),
            )
        )
    )
    clean, gains, consensus = pl.pallas_call(
        store_kernel,
        out_shape=shapes,
        in_specs=[vmem] * 3,
        out_specs=(anywhere, anywhere, anywhere),
        scratch_shapes=[pltpu.SemaphoreType.DMA((2 + 2 * chan_dev,))],
        compiler_params=pltpu.CompilerParams(vmem_limit_bytes=8 * 1024 * 1024),
    )(*results)
    return clean, gains, consensus.reshape(CL)


def solution(mesh):
    placed = (P(None, "chan", "bl", None), P("bl", None), P(), P(), P(), P(), P("bl", None, None))
    return jax.shard_map(
        per_device,
        mesh=mesh,
        in_specs=placed,
        out_specs=(P(None, "chan", "bl", None), P("bl", None), P()),
        check_vma=False,
    )
```

```python
import functools

import jax
import jax.numpy as jnp
from jax import lax
from jax.experimental import pallas as pl
from jax.experimental.pallas import tpu as pltpu
from jax.sharding import PartitionSpec as P

CL = 12
SUB_ITERS = 3
ADMM_ITERS = 6
PHASE_SCALE = 20.0
RHO_SCALE = 0.5

HIGHEST = lax.Precision.HIGHEST
MESH = pl.DeviceIdType.MESH
F32 = jnp.float32
BF16 = jnp.bfloat16
LANES = 128
GROUP = 16
NT = (((1,), (1,)), ((), ()))
TN = (((0,), (0,)), ((), ()))


def split3(x):
    a = x.astype(BF16).astype(F32)
    rest = x - a
    b = rest.astype(BF16).astype(F32)
    return a, b, rest - b


def sincos(phase):
    k = jnp.floor(phase * F32(0.6366197723675814) + F32(0.5))
    r = phase - k * F32(1.5703125)
    r = r - k * F32(4.837512969970703125e-4)
    r = r - k * F32(7.54978995489188216e-8)
    r2 = r * r
    s = r + r * r2 * (F32(-1.6666654611e-1) + r2 * (F32(8.3321608736e-3) + r2 * F32(-1.9515295891e-4)))
    c = (F32(1.0) - F32(0.5) * r2) + r2 * r2 * (
        F32(4.166664568298827e-2) + r2 * (F32(-1.388731625493765e-3) + r2 * F32(2.443315711809948e-5))
    )
    ki = k.astype(jnp.int32)
    odd = (ki & 1) == 1
    cos = jnp.where(odd, s, c)
    sin = jnp.where(odd, c, s)
    cos = jnp.where(((ki + 1) & 2) == 2, -cos, cos)
    sin = jnp.where((ki & 2) == 2, -sin, sin)
    return cos, sin


def orthonormal(rows):
    count = rows.shape[1]
    sub = lax.broadcasted_iota(jnp.int32, (1, count, 1), 1)
    cols = [jnp.sum(rows * rows[:, k : k + 1, :], axis=-1, keepdims=True) for k in range(count)]
    square = cols[0][:, 0:1, :]
    for k in range(count):
        pivot = cols[k][:, k : k + 1, :]
        square = jnp.where(sub == k, pivot, square)
        if k == count - 1:
            break
        ratio = jnp.where(sub > k, cols[k] * (F32(1.0) / pivot), F32(0.0))
        for m in range(k + 1, count):
            cols[m] = cols[m] - ratio * cols[m][:, k : k + 1, :]
        rows = rows - ratio * rows[:, k : k + 1, :]
    return rows * lax.rsqrt(square)


def main_kernel(
    n_chan, n_bl, channels,
    vis_hbm, pair_hbm, coords_hbm, lm_hbm, tb_hbm, cluster_hbm, seed_hbm,
    clean_ref, gains_ref, cons_ref,
    vis_ref, pair_ref, coords_ref, lm_ref, tb_ref, cluster_ref, seed_ref,
    gsplit, resp, lmp, tbp, clp, coord_rows, uv_ref, bsplit, tsplit, qsplit, before_ref, spread,
    ybuf, nbuf, mbuf, vbuf, lbuf, send_sems, recv_sems, vis_sems, load_sems,
):
    chan_dev, base_dev, times = vis_ref.shape[1:]
    tiles, rank = seed_ref.shape[0], seed_ref.shape[1]
    tile = base_dev // tiles
    dirs = tb_ref.shape[0]
    dpad = tbp.shape[0]
    stations = coords_ref.shape[1]
    n_all = n_chan * n_bl
    tiles_all = tiles * n_bl
    my_chan = lax.axis_index("chan")
    my_bl = lax.axis_index("bl")
    my_id = my_chan * n_bl + my_bl

    loads = [
        pltpu.make_async_copy(src, dst, load_sems.at[i])
        for i, (src, dst) in enumerate(
            (
                (seed_hbm, seed_ref),
                (pair_hbm, pair_ref),
                (coords_hbm, coords_ref),
                (lm_hbm, lm_ref),
                (tb_hbm, tb_ref),
                (cluster_hbm, cluster_ref),
            )
        )
    ]
    vis_loads = []
    for j in range(tiles):
        at = (slice(None), slice(None), pl.ds(j * tile, tile), slice(None))
        vis_loads.append(pltpu.make_async_copy(vis_hbm.at[at], vis_ref.at[at], vis_sems.at[j]))
    loads[0].start()
    for load in vis_loads:
        load.start()
    for load in loads[1:]:
        load.start()

    def everyone(off):
        other = lax.rem(my_id + off, n_all)
        return (lax.div(other, n_bl), lax.rem(other, n_bl))

    def along_chan(off):
        return (lax.rem(my_chan + off, n_chan), my_bl)

    def along_bl(off):
        return (my_chan, lax.rem(my_bl + off, n_bl))

    barrier = pltpu.get_barrier_semaphore()

    @pl.loop(1, n_all)
    def _(off):
        pl.semaphore_signal(barrier, inc=1, device_id=everyone(off), device_id_type=MESH)

    def push(buf, me, n, peer, phase):
        @pl.loop(1, n)
        def _(off):
            pltpu.make_async_remote_copy(
                src_ref=buf.at[me],
                dst_ref=buf.at[me],
                send_sem=send_sems.at[phase],
                recv_sem=recv_sems.at[phase],
                device_id=peer(off),
                device_id_type=MESH,
            ).start()

    def push_rows(step, j):
        @pl.loop(1, n_chan)
        def _(off):
            part = ybuf.at[step, my_chan, pl.ds(j * rank, rank)]
            pltpu.make_async_remote_copy(
                src_ref=part,
                dst_ref=part,
                send_sem=send_sems.at[step],
                recv_sem=recv_sems.at[step],
                device_id=along_chan(off),
                device_id_type=MESH,
            ).start()

    def arrived(buf, n, phase):
        part = buf.at[pl.ds(0, n - 1)]
        pltpu.make_async_copy(part, part, recv_sems.at[phase]).wait()

    def sent(buf, n, phase):
        part = buf.at[pl.ds(0, n - 1)]
        pltpu.make_async_copy(part, part, send_sems.at[phase]).wait()

    def total(buf, n):
        out = buf[0]
        for i in range(1, n):
            out = out + buf[i]
        return out

    def vis_tile(j):
        return vis_ref[:, :, j * tile : (j + 1) * tile, :].reshape(2 * chan_dev * tile, times)

    def seen(j):
        seed = seed_ref[j].astype(F32)
        seed = jnp.concatenate([seed, jnp.zeros_like(seed)], axis=0).astype(BF16)
        p1, p2, p3 = split3(lax.dot_general(seed, vis_tile(j), NT, preferred_element_type=F32)[:rank])
        return jnp.concatenate([p1, p2, p3, jnp.zeros_like(p1)], axis=0).astype(BF16)

    def back(lhs, j):
        acc = jnp.dot(lhs, vis_tile(j), preferred_element_type=F32)
        ybuf[0, my_chan, j * rank : (j + 1) * rank] = acc[:rank] + (acc[rank : 2 * rank] + acc[2 * rank : 3 * rank])

    loads[0].wait()
    held = None
    for j in range(tiles):
        vis_loads[j].wait()
        lhs = seen(j)
        if j:
            back(held, j - 1)
        held = lhs
    back(held, tiles - 1)
    pl.semaphore_wait(barrier, n_all - 1)
    push(ybuf.at[0], my_chan, n_chan, along_chan, 0)

    for load in loads[1:]:
        load.wait()
    lmp[...] = jnp.zeros_like(lmp)
    lmp[0:2, 0:dirs] = lm_ref[...]
    tbp[...] = jnp.zeros_like(tbp)
    tbp[0:dirs, :] = tb_ref[...]
    clp[...] = jnp.full_like(clp, -1)
    clp[0:1, 0:dirs] = cluster_ref[...]
    c1, c2, c3 = split3(coords_ref[...])
    coord_rows[...] = jnp.zeros_like(coord_rows)
    coord_rows[0:2, :] = c1
    coord_rows[2:4, :] = c2
    coord_rows[4:6, :] = c3
    tb = tbp[...]
    beam_gram = lax.dot_general(tb, tb, NT, precision=HIGHEST, preferred_element_type=F32)
    member = jnp.where(
        lax.broadcasted_iota(jnp.int32, (LANES, dpad), 0) == clp[0:1, 0:dpad], F32(1.0), F32(0.0)
    )
    named = jnp.broadcast_to(clp[0:1, :].astype(F32), (LANES, LANES)).T[0:dpad]
    lane_group = lax.rem(lax.div(lax.broadcasted_iota(jnp.int32, (dpad, LANES), 1), GROUP), tiles)
    for m in range(CL):
        hit = jnp.where(named == F32(m), F32(1.0), F32(0.0))
        for j in range(tiles):
            spread[j * dpad : (j + 1) * dpad, m * LANES : (m + 1) * LANES] = jnp.where(
                lane_group == j, hit, F32(0.0)
            ).astype(BF16)
    station = lax.broadcasted_iota(jnp.int32, (stations, base_dev), 0)
    pick = jnp.where(station == pair_ref[0:1, :], F32(1.0), F32(0.0)) - jnp.where(
        station == pair_ref[1:2, :], F32(1.0), F32(0.0)
    )
    uv_ref[...] = jnp.dot(coord_rows[...].astype(BF16), pick.astype(BF16), preferred_element_type=F32)
    uv = uv_ref[0:2, :] + uv_ref[2:4, :] + uv_ref[4:6, :]
    uv_ref[0:2, :] = uv
    uv_ref[2:8, :] = jnp.zeros((6, base_dev), F32)
    geo = lax.dot_general(
        lmp[:, 0:dpad], uv_ref[0:8, :], TN, precision=HIGHEST, preferred_element_type=F32
    )
    for j in range(tiles):
        v = vis_tile(j)
        gram = lax.dot_general(v, v, TN, preferred_element_type=F32)
        g1, g2, g3 = split3(gram)
        gsplit[j, 0] = g1.astype(BF16)
        gsplit[j, 1] = g2.astype(BF16)
        gsplit[j, 2] = g3.astype(BF16)
    opening = (my_chan * chan_dev).astype(F32) * F32(PHASE_SCALE / channels) + F32(PHASE_SCALE)
    for j in range(tiles):
        part = geo[:, j * tile : (j + 1) * tile]
        cos, sin = sincos(opening * part)
        cos_step, sin_step = sincos(F32(PHASE_SCALE / channels) * part)
        for c in range(chan_dev):
            if c:
                cos, sin = cos * cos_step - sin * sin_step, sin * cos_step + cos * sin_step
            resp[j, :, c * tile : (c + 1) * tile] = cos.astype(BF16)
            resp[j, :, (chan_dev + c) * tile : (chan_dev + c + 1) * tile] = sin.astype(BF16)

    member_rows = member[0:GROUP]
    halves = []
    for j in range(tiles):
        r = resp[j]
        model = lax.dot_general(r, r, NT, preferred_element_type=F32)
        halves.append(jnp.dot(member_rows, model * beam_gram, precision=HIGHEST, preferred_element_type=F32))
    nbuf[my_chan] = jnp.concatenate(halves, axis=1)
    push(nbuf, my_chan, n_chan, along_chan, SUB_ITERS)

    def advance(block, step):
        for j in range(tiles):
            z1, z2, z3 = split3(block[j])
            lhs = jnp.concatenate([z1, z2, z3, jnp.zeros_like(z1)], axis=0).astype(BF16)
            p1 = jnp.dot(lhs, gsplit[j, 0], preferred_element_type=F32)
            p2 = jnp.dot(lhs[: 2 * rank], gsplit[j, 1], preferred_element_type=F32)
            p3 = jnp.dot(lhs[: 2 * rank], gsplit[j, 2], preferred_element_type=F32)
            low = p1[2 * rank : 3 * rank] + p2[rank : 2 * rank] + p3[:rank]
            ybuf[step, my_chan, j * rank : (j + 1) * rank] = p1[:rank] + (p1[rank : 2 * rank] + p2[:rank] + low)
            push_rows(step, j)

    def gathered(step):
        arrived(ybuf.at[step], n_chan, step)
        return orthonormal(total(ybuf.at[step], n_chan).reshape(tiles, rank, times))

    advance(gathered(0), 1)

    weighted = []
    for j in range(tiles):
        at = slice(j * dpad, (j + 1) * dpad)
        bp = jnp.dot(resp[j], vis_tile(j), preferred_element_type=F32)
        weighted.append(bp * tb)
        for ref, part in ((bsplit, bp), (tsplit, tb)):
            b1, b2, b3 = split3(part)
            ref[0, at] = b1.astype(BF16)
            ref[1, at] = b2.astype(BF16)
            ref[2, at] = b3.astype(BF16)

    arrived(nbuf, n_chan, SUB_ITERS)
    sub = lax.broadcasted_iota(jnp.int32, (GROUP, LANES), 0)
    lane = lax.broadcasted_iota(jnp.int32, (GROUP, LANES), 1)
    eye = jnp.where(sub == lane, F32(1.0), F32(0.0))
    n1, n2, n3 = split3(total(nbuf, n_chan))
    lhs = jnp.concatenate([n1, n2, n3], axis=0).astype(BF16)
    wide = jnp.dot(lhs, spread[...], preferred_element_type=F32)
    wide = wide[:GROUP] + (wide[GROUP : 2 * GROUP] + wide[2 * GROUP :])
    cols = [wide[:, m * LANES : (m + 1) * LANES] for m in range(CL)]
    trace = cols[0][0:1]
    for m in range(1, CL):
        trace = trace + cols[m][m : m + 1]
    recip = F32(1.0) / (F32(RHO_SCALE) * trace / F32(CL))
    inv_rho = [recip[:, j * GROUP : j * GROUP + 1] for j in range(tiles)]
    cols = [jnp.where(sub == m, F32(1.0), F32(0.0)) + cols[m] * recip for m in range(CL)]
    for p in range(CL):
        col = cols[p]
        d = F32(1.0) / col[p : p + 1]
        for m in range(CL):
            if m != p:
                f = cols[m][p : p + 1] * d
                cols[m] = jnp.where(sub == p, f, cols[m] - col * f)
        cols[p] = jnp.where(sub == p, d, -col * d)
    first = jnp.zeros((GROUP, LANES), F32)
    for m in range(CL):
        here = (lax.rem(lane, GROUP) == m) & (lane < tiles * GROUP)
        first = jnp.where(here, jnp.where(sub == m, F32(1.0), F32(0.0)) - cols[m], first)

    def times_of(a, b):
        return jnp.dot(a, b, precision=HIGHEST, preferred_element_type=F32)

    def blocks(m):
        rows = [jnp.where(lax.div(lane, GROUP) == j, m, F32(0.0)) for j in range(tiles)]
        return jnp.concatenate(rows + [jnp.zeros((LANES - tiles * GROUP, LANES), F32)], axis=0)

    advance(gathered(1), 2)

    e1 = blocks(first)
    second = times_of(first, e1)
    e2 = blocks(second)
    third = times_of(second, e1)
    later = times_of(jnp.concatenate([second, third], axis=0), e2)
    powers = [first, second, third, later[:GROUP], later[GROUP:], times_of(later[:GROUP], e2)]
    group = lax.div(lane, GROUP)
    by_tile = []
    for j in range(tiles):
        out = jnp.zeros((GROUP, LANES), F32)
        for p in range(ADMM_ITERS):
            shift = (p - j) * GROUP % LANES
            m = pltpu.roll(powers[p], shift, 1) if shift else powers[p]
            out = jnp.where(group == p, m, out)
        by_tile.append(out)
    packed = by_tile[0]
    for j in range(1, tiles):
        packed = packed + by_tile[j]
    mbuf[my_bl] = packed
    push(mbuf, my_bl, n_bl, along_bl, SUB_ITERS + 1)
    eye_all = jnp.where(lax.rem(lane, GROUP) == sub, F32(1.0), F32(0.0))
    eye_all = jnp.where(lane < tiles * GROUP, eye_all, F32(0.0))
    powers = [eye_all] + powers

    before_ref[...] = lax.dot_general(
        jnp.ones((8, times), F32), jnp.concatenate(weighted, axis=0), NT, precision=HIGHEST, preferred_element_type=F32
    )
    eye_rep = jnp.where((lax.rem(lane, GROUP) == sub) & (group < ADMM_ITERS), F32(1.0), F32(0.0))
    final = powers[ADMM_ITERS - 1] - powers[ADMM_ITERS]
    for j in range(tiles):
        own = jnp.where(group == j, final, F32(0.0))
        both = jnp.concatenate([eye_rep - by_tile[j], own], axis=1) * inv_rho[j]
        q1, q2, q3 = split3(
            lax.dot_general(member_rows, both, TN, precision=HIGHEST, preferred_element_type=F32)
        )
        at = slice(j * dpad, (j + 1) * dpad)
        qsplit[0, at] = q1.astype(BF16)
        qsplit[1, at] = q2.astype(BF16)
        qsplit[2, at] = q3.astype(BF16)

    def stacked(row):
        a, b, c = split3(row)
        at = lax.broadcasted_iota(jnp.int32, (16, row.shape[1]), 0)
        return jnp.where(at == 0, a, jnp.where(at == 1, b, jnp.where(at == 2, c, F32(0.0)))).astype(BF16)

    def row_times(row, parts):
        lhs = stacked(row)
        at = lax.broadcasted_iota(jnp.int32, (16, parts[0].shape[1]), 0)
        acc = jnp.where(at < 1, jnp.dot(lhs, parts[2], preferred_element_type=F32), F32(0.0))
        acc = acc + jnp.where(at < 2, jnp.dot(lhs, parts[1], preferred_element_type=F32), F32(0.0))
        acc = acc + jnp.where(at < 3, jnp.dot(lhs, parts[0], preferred_element_type=F32), F32(0.0))
        return jnp.sum(acc, axis=0, keepdims=True)

    def along_times(lhs, ref):
        acc = lax.dot_general(lhs, ref[2], NT, preferred_element_type=F32)
        acc = acc + lax.dot_general(lhs, ref[1], NT, preferred_element_type=F32)
        return acc + lax.dot_general(lhs, ref[0], NT, preferred_element_type=F32)

    basis = gathered(2).astype(BF16).astype(F32).reshape(tiles * rank, times)
    rows16 = basis.astype(BF16)
    product = along_times(rows16, bsplit) * along_times(rows16, tsplit)
    row_tile = lax.div(lax.broadcasted_iota(jnp.int32, product.shape, 0), rank)
    lane_tile = lax.div(lax.broadcasted_iota(jnp.int32, product.shape, 1), dpad)
    product = jnp.where(row_tile == lane_tile, product, F32(0.0))
    rhs_row = before_ref[0:1] - jnp.sum(product, axis=0, keepdims=True)
    row = row_times(rhs_row, (qsplit[0], qsplit[1], qsplit[2]))
    vbuf[my_id] = row[:, 0:LANES]
    lbuf[my_chan] = row[:, LANES : 2 * LANES]
    push(vbuf, my_id, n_all, everyone, SUB_ITERS + 2)
    push(lbuf, my_chan, n_chan, along_chan, SUB_ITERS + 3)

    part_lane = lax.broadcasted_iota(jnp.int32, (1, 4 * rank), 1)
    for j in range(tiles):
        own = basis[j * rank : (j + 1) * rank]
        wide = jnp.concatenate([own, own, own, jnp.zeros_like(own)], axis=0).astype(BF16)
        v = vis_tile(j)
        proj = lax.dot_general(v, wide, NT, preferred_element_type=F32)
        a, b, c = split3(proj)
        parts = jnp.where(part_lane < rank, a, jnp.where(part_lane < 2 * rank, b, c)).astype(BF16)
        correction = jnp.dot(parts, wide, preferred_element_type=F32)
        clean_ref[:, :, j * tile : (j + 1) * tile, :] = (
            (v.astype(F32) - correction).astype(BF16).reshape(2, chan_dev, tile, times)
        )

    arrived(mbuf, n_bl, SUB_ITERS + 1)
    moments = jnp.where(group < ADMM_ITERS - 1, total(mbuf, n_bl) * F32(1.0 / tiles_all), F32(0.0))
    history = jnp.where(group == 0, eye, pltpu.roll(moments, GROUP, 1))
    gain = jnp.where(group < ADMM_ITERS - 1, history, F32(0.0)) - F32(2.0) * moments
    local = []
    for i in range(1, ADMM_ITERS - 1):
        k = ADMM_ITERS - 2 - i
        local.append(F32(3.0) * powers[k + 1] - powers[k] - F32(2.0) * powers[k + 2])
    local.append(F32(2.0) * (powers[0] - powers[1]))
    apply = [jnp.where(lane == sub + tiles * GROUP, F32(1.0), F32(0.0))]
    for k in range(ADMM_ITERS - 2, -1, -1):
        pad = jnp.zeros((LANES - len(apply) * GROUP, LANES), F32)
        apply.insert(0, local[k] + times_of(gain, jnp.concatenate(apply + [pad], axis=0)))
    factor = F32((channels * tile * times) ** 0.5)
    pad = jnp.zeros((LANES - len(apply) * GROUP, LANES), F32)
    apply = jnp.concatenate(apply + [pad], axis=0) * F32((channels * tile * times) ** 0.5 / tiles_all)
    parts = tuple(part.astype(BF16) for part in split3(apply))
    arrived(vbuf, n_all, SUB_ITERS + 2)
    arrived(lbuf, n_chan, SUB_ITERS + 3)
    x = row_times(total(vbuf, n_all), parts) + total(lbuf, n_chan) * factor
    x = jnp.broadcast_to(x, (8, LANES))
    for j in range(tiles):
        at = x if j == 0 else pltpu.roll(x, LANES - j * GROUP, 1)
        gains_ref[j : j + 1, :] = at[0:1, 0:CL]
    cons_ref[...] = pltpu.roll(x, LANES - tiles * GROUP, 1)[0:1, 0:CL]

    for step in range(SUB_ITERS):
        sent(ybuf.at[step], n_chan, step)
    sent(nbuf, n_chan, SUB_ITERS)
    sent(mbuf, n_bl, SUB_ITERS + 1)
    sent(vbuf, n_all, SUB_ITERS + 2)
    sent(lbuf, n_chan, SUB_ITERS + 3)


def store_kernel(clean_in, gains_in, cons_in, clean_out, gains_out, cons_out, sems):
    parts, chans = clean_in.shape[:2]
    stores = [
        pltpu.make_async_copy(gains_in, gains_out, sems.at[0]),
        pltpu.make_async_copy(cons_in, cons_out, sems.at[1]),
    ]
    for p in range(parts):
        for c in range(chans):
            stores.append(
                pltpu.make_async_copy(clean_in.at[p, c], clean_out.at[p, c], sems.at[2 + p * chans + c])
            )
    for store in stores:
        store.start()
    for store in stores:
        store.wait()


def per_device(vis, station_pair_index, station_coords, dir_lm, time_beam, dir_cluster, seed_block):
    n_chan = lax.axis_size("chan")
    n_bl = lax.axis_size("bl")
    chan_dev, base_dev, times = vis.shape[1:]
    tiles, _, rank = seed_block.shape
    tile = base_dev // tiles
    dirs = dir_lm.shape[0]
    dpad = (dirs + 15) // 16 * 16
    stations = station_coords.shape[0]
    vmem = pl.BlockSpec(memory_space=pltpu.VMEM)
    anywhere = pl.BlockSpec(memory_space=pl.ANY)
    shapes = (
        jax.ShapeDtypeStruct(vis.shape, BF16),
        jax.ShapeDtypeStruct((tiles, CL), F32),
        jax.ShapeDtypeStruct((1, CL), F32),
    )
    results = pl.pallas_call(
        functools.partial(main_kernel, n_chan, n_bl, chan_dev * n_chan),
        out_shape=tuple(pltpu.VMEM(s.shape, s.dtype) for s in shapes),
        in_specs=[anywhere] * 7,
        out_specs=(vmem, vmem, vmem),
        scratch_shapes=[
            pltpu.VMEM(vis.shape, BF16),
            pltpu.VMEM((2, base_dev), jnp.int32),
            pltpu.VMEM((2, stations), F32),
            pltpu.VMEM((2, dirs), F32),
            pltpu.VMEM((dirs, times), F32),
            pltpu.VMEM((1, dirs), jnp.int32),
            pltpu.VMEM((tiles, rank, times), jnp.int32),
            pltpu.VMEM((tiles, 3, times, times), BF16),
            pltpu.VMEM((tiles, dpad, 2 * chan_dev * tile), BF16),
            pltpu.VMEM((8, LANES), F32),
            pltpu.VMEM((dpad, times), F32),
            pltpu.VMEM((8, LANES), jnp.int32),
            pltpu.VMEM((GROUP, stations), F32),
            pltpu.VMEM((GROUP, base_dev), F32),
            pltpu.VMEM((3, tiles * dpad, times), BF16),
            pltpu.VMEM((3, tiles * dpad, times), BF16),
            pltpu.VMEM((3, tiles * dpad, 2 * LANES), BF16),
            pltpu.VMEM((8, tiles * dpad), F32),
            pltpu.VMEM((tiles * dpad, CL * LANES), BF16),
            pltpu.VMEM((SUB_ITERS, n_chan, tiles * rank, times), F32),
            pltpu.VMEM((n_chan, GROUP, tiles * dpad), F32),
            pltpu.VMEM((n_bl, GROUP, LANES), F32),
            pltpu.VMEM((n_chan * n_bl, 1, LANES), F32),
            pltpu.VMEM((n_chan, 1, LANES), F32),
            pltpu.SemaphoreType.DMA((SUB_ITERS + 4,)),
            pltpu.SemaphoreType.DMA((SUB_ITERS + 4,)),
            pltpu.SemaphoreType.DMA((tiles,)),
            pltpu.SemaphoreType.DMA((6,)),
        ],
        compiler_params=pltpu.CompilerParams(
            collective_id=0, has_side_effects=True, vmem_limit_bytes=32 * 1024 * 1024
        ),
    )(
        *(
            pltpu.with_memory_space_constraint(a, pltpu.HBM)
            for a in (
                vis,
                station_pair_index.T,
                station_coords.T,
                dir_lm.T,
                time_beam,
                dir_cluster.reshape(1, dirs),
                jnp.swapaxes(seed_block, 1, 2),
            )
        )
    )
    clean, gains, consensus = pl.pallas_call(
        store_kernel,
        out_shape=shapes,
        in_specs=[vmem] * 3,
        out_specs=(anywhere, anywhere, anywhere),
        scratch_shapes=[pltpu.SemaphoreType.DMA((2 + 2 * chan_dev,))],
        compiler_params=pltpu.CompilerParams(vmem_limit_bytes=8 * 1024 * 1024),
    )(*results)
    return clean, gains, consensus.reshape(CL)


def solution(mesh):
    placed = (P(None, "chan", "bl", None), P("bl", None), P(), P(), P(), P(), P("bl", None, None))
    return jax.shard_map(
        per_device,
        mesh=mesh,
        in_specs=placed,
        out_specs=(P(None, "chan", "bl", None), P("bl", None), P()),
        check_vma=False,
    )
```

```python
import functools

import jax
import jax.numpy as jnp
from jax import lax
from jax.experimental import pallas as pl
from jax.experimental.pallas import tpu as pltpu
from jax.sharding import PartitionSpec as P

CL = 12
SUB_ITERS = 3
ADMM_ITERS = 6
PHASE_SCALE = 20.0
RHO_SCALE = 0.5

HIGHEST = lax.Precision.HIGHEST
MESH = pl.DeviceIdType.MESH
F32 = jnp.float32
BF16 = jnp.bfloat16
LANES = 128
GROUP = 16
NT = (((1,), (1,)), ((), ()))
TN = (((0,), (0,)), ((), ()))


def split3(x):
    a = x.astype(BF16).astype(F32)
    rest = x - a
    b = rest.astype(BF16).astype(F32)
    return a, b, rest - b


def sincos(phase):
    k = jnp.floor(phase * F32(0.6366197723675814) + F32(0.5))
    r = phase - k * F32(1.5703125)
    r = r - k * F32(4.837512969970703125e-4)
    r = r - k * F32(7.54978995489188216e-8)
    r2 = r * r
    s = r + r * r2 * (F32(-1.6666654611e-1) + r2 * (F32(8.3321608736e-3) + r2 * F32(-1.9515295891e-4)))
    c = (F32(1.0) - F32(0.5) * r2) + r2 * r2 * (
        F32(4.166664568298827e-2) + r2 * (F32(-1.388731625493765e-3) + r2 * F32(2.443315711809948e-5))
    )
    ki = k.astype(jnp.int32)
    odd = (ki & 1) == 1
    cos = jnp.where(odd, s, c)
    sin = jnp.where(odd, c, s)
    cos = jnp.where(((ki + 1) & 2) == 2, -cos, cos)
    sin = jnp.where((ki & 2) == 2, -sin, sin)
    return cos, sin


def orthonormal(rows):
    count = rows.shape[1]
    sub = lax.broadcasted_iota(jnp.int32, (1, count, 1), 1)
    cols = [jnp.sum(rows * rows[:, k : k + 1, :], axis=-1, keepdims=True) for k in range(count)]
    square = cols[0][:, 0:1, :]
    for k in range(count):
        pivot = cols[k][:, k : k + 1, :]
        square = jnp.where(sub == k, pivot, square)
        if k == count - 1:
            break
        ratio = jnp.where(sub > k, cols[k] * (F32(1.0) / pivot), F32(0.0))
        for m in range(k + 1, count):
            cols[m] = cols[m] - ratio * cols[m][:, k : k + 1, :]
        rows = rows - ratio * rows[:, k : k + 1, :]
    return rows * lax.rsqrt(square)


def main_kernel(
    n_chan, n_bl, channels,
    vis_hbm, pair_hbm, coords_hbm, lm_hbm, tb_hbm, cluster_hbm, seed_hbm,
    clean_ref, gains_ref, cons_ref,
    vis_ref, pair_ref, coords_ref, lm_ref, tb_ref, cluster_ref, seed_ref,
    gsplit, resp, lmp, tbp, clp, coord_rows, uv_ref, bsplit, tsplit, qsplit, before_ref, spread,
    ybuf, nbuf, mbuf, vbuf, lbuf, send_sems, recv_sems, vis_sems, load_sems,
):
    chan_dev, base_dev, times = vis_ref.shape[1:]
    tiles, rank = seed_ref.shape[0], seed_ref.shape[1]
    tile = base_dev // tiles
    dirs = tb_ref.shape[0]
    dpad = tbp.shape[0]
    stations = coords_ref.shape[1]
    n_all = n_chan * n_bl
    tiles_all = tiles * n_bl
    my_chan = lax.axis_index("chan")
    my_bl = lax.axis_index("bl")
    my_id = my_chan * n_bl + my_bl

    loads = [
        pltpu.make_async_copy(src, dst, load_sems.at[i])
        for i, (src, dst) in enumerate(
            (
                (seed_hbm, seed_ref),
                (pair_hbm, pair_ref),
                (coords_hbm, coords_ref),
                (lm_hbm, lm_ref),
                (tb_hbm, tb_ref),
                (cluster_hbm, cluster_ref),
            )
        )
    ]
    vis_loads = []
    for j in range(tiles):
        at = (slice(None), slice(None), pl.ds(j * tile, tile), slice(None))
        vis_loads.append(pltpu.make_async_copy(vis_hbm.at[at], vis_ref.at[at], vis_sems.at[j]))
    loads[0].start()
    for load in vis_loads:
        load.start()
    for load in loads[1:]:
        load.start()

    def everyone(off):
        other = lax.rem(my_id + off, n_all)
        return (lax.div(other, n_bl), lax.rem(other, n_bl))

    def along_chan(off):
        return (lax.rem(my_chan + off, n_chan), my_bl)

    def along_bl(off):
        return (my_chan, lax.rem(my_bl + off, n_bl))

    barrier = pltpu.get_barrier_semaphore()

    @pl.loop(1, n_all)
    def _(off):
        pl.semaphore_signal(barrier, inc=1, device_id=everyone(off), device_id_type=MESH)

    def push(buf, me, n, peer, phase):
        @pl.loop(1, n)
        def _(off):
            pltpu.make_async_remote_copy(
                src_ref=buf.at[me],
                dst_ref=buf.at[me],
                send_sem=send_sems.at[phase],
                recv_sem=recv_sems.at[phase],
                device_id=peer(off),
                device_id_type=MESH,
            ).start()

    def push_rows(step, j):
        @pl.loop(1, n_chan)
        def _(off):
            part = ybuf.at[step, my_chan, pl.ds(j * rank, rank)]
            pltpu.make_async_remote_copy(
                src_ref=part,
                dst_ref=part,
                send_sem=send_sems.at[step],
                recv_sem=recv_sems.at[step],
                device_id=along_chan(off),
                device_id_type=MESH,
            ).start()

    def arrived(buf, n, phase):
        part = buf.at[pl.ds(0, n - 1)]
        pltpu.make_async_copy(part, part, recv_sems.at[phase]).wait()

    def sent(buf, n, phase):
        part = buf.at[pl.ds(0, n - 1)]
        pltpu.make_async_copy(part, part, send_sems.at[phase]).wait()

    def total(buf, n):
        out = buf[0]
        for i in range(1, n):
            out = out + buf[i]
        return out

    def tree(buf, n):
        rows = [buf[i] for i in range(n)]
        while len(rows) > 1:
            rows = [rows[i] + rows[i + 1] if i + 1 < len(rows) else rows[i] for i in range(0, len(rows), 2)]
        return rows[0]

    def vis_tile(j):
        return vis_ref[:, :, j * tile : (j + 1) * tile, :].reshape(2 * chan_dev * tile, times)

    def seen(j):
        seed = seed_ref[j].astype(F32)
        seed = jnp.concatenate([seed, jnp.zeros_like(seed)], axis=0).astype(BF16)
        p1, p2, p3 = split3(lax.dot_general(seed, vis_tile(j), NT, preferred_element_type=F32)[:rank])
        return jnp.concatenate([p1, p2, p3, jnp.zeros_like(p1)], axis=0).astype(BF16)

    def back(lhs, j):
        acc = jnp.dot(lhs, vis_tile(j), preferred_element_type=F32)
        ybuf[0, my_chan, j * rank : (j + 1) * rank] = acc[:rank] + (acc[rank : 2 * rank] + acc[2 * rank : 3 * rank])

    loads[0].wait()
    held = None
    for j in range(tiles):
        vis_loads[j].wait()
        lhs = seen(j)
        if j:
            back(held, j - 1)
        held = lhs
    back(held, tiles - 1)
    pl.semaphore_wait(barrier, n_all - 1)
    push(ybuf.at[0], my_chan, n_chan, along_chan, 0)

    for load in loads[1:]:
        load.wait()
    lmp[...] = jnp.zeros_like(lmp)
    lmp[0:2, 0:dirs] = lm_ref[...]
    tbp[...] = jnp.zeros_like(tbp)
    tbp[0:dirs, :] = tb_ref[...]
    clp[...] = jnp.full_like(clp, -1)
    clp[0:1, 0:dirs] = cluster_ref[...]
    c1, c2, c3 = split3(coords_ref[...])
    coord_rows[...] = jnp.zeros_like(coord_rows)
    coord_rows[0:2, :] = c1
    coord_rows[2:4, :] = c2
    coord_rows[4:6, :] = c3
    tb = tbp[...]
    beam_gram = lax.dot_general(tb, tb, NT, precision=HIGHEST, preferred_element_type=F32)
    member = jnp.where(
        lax.broadcasted_iota(jnp.int32, (LANES, dpad), 0) == clp[0:1, 0:dpad], F32(1.0), F32(0.0)
    )
    named = jnp.broadcast_to(clp[0:1, :].astype(F32), (LANES, LANES)).T[0:dpad]
    lane_group = lax.rem(lax.div(lax.broadcasted_iota(jnp.int32, (dpad, LANES), 1), GROUP), tiles)
    for m in range(CL):
        hit = jnp.where(named == F32(m), F32(1.0), F32(0.0))
        for j in range(tiles):
            spread[j * dpad : (j + 1) * dpad, m * LANES : (m + 1) * LANES] = jnp.where(
                lane_group == j, hit, F32(0.0)
            ).astype(BF16)
    station = lax.broadcasted_iota(jnp.int32, (stations, base_dev), 0)
    pick = jnp.where(station == pair_ref[0:1, :], F32(1.0), F32(0.0)) - jnp.where(
        station == pair_ref[1:2, :], F32(1.0), F32(0.0)
    )
    uv_ref[...] = jnp.dot(coord_rows[...].astype(BF16), pick.astype(BF16), preferred_element_type=F32)
    uv = uv_ref[0:2, :] + uv_ref[2:4, :] + uv_ref[4:6, :]
    uv_ref[0:2, :] = uv
    uv_ref[2:8, :] = jnp.zeros((6, base_dev), F32)
    geo = lax.dot_general(
        lmp[:, 0:dpad], uv_ref[0:8, :], TN, precision=HIGHEST, preferred_element_type=F32
    )
    for j in range(tiles):
        v = vis_tile(j)
        gram = lax.dot_general(v, v, TN, preferred_element_type=F32)
        g1, g2, g3 = split3(gram)
        gsplit[j, 0] = g1.astype(BF16)
        gsplit[j, 1] = g2.astype(BF16)
        gsplit[j, 2] = g3.astype(BF16)
    opening = (my_chan * chan_dev).astype(F32) * F32(PHASE_SCALE / channels) + F32(PHASE_SCALE)
    for j in range(tiles):
        part = geo[:, j * tile : (j + 1) * tile]
        cos, sin = sincos(opening * part)
        cos_step, sin_step = sincos(F32(PHASE_SCALE / channels) * part)
        for c in range(chan_dev):
            if c:
                cos, sin = cos * cos_step - sin * sin_step, sin * cos_step + cos * sin_step
            resp[j, :, c * tile : (c + 1) * tile] = cos.astype(BF16)
            resp[j, :, (chan_dev + c) * tile : (chan_dev + c + 1) * tile] = sin.astype(BF16)

    member_rows = member[0:GROUP]
    halves = []
    for j in range(tiles):
        r = resp[j]
        model = lax.dot_general(r, r, NT, preferred_element_type=F32)
        halves.append(jnp.dot(member_rows, model * beam_gram, precision=HIGHEST, preferred_element_type=F32))
    nbuf[my_chan] = jnp.concatenate(halves, axis=1)
    push(nbuf, my_chan, n_chan, along_chan, SUB_ITERS)

    def advance(block, step):
        for j in range(tiles):
            z1, z2, z3 = split3(block[j])
            lhs = jnp.concatenate([z1, z2, z3, jnp.zeros_like(z1)], axis=0).astype(BF16)
            p1 = jnp.dot(lhs, gsplit[j, 0], preferred_element_type=F32)
            p2 = jnp.dot(lhs[: 2 * rank], gsplit[j, 1], preferred_element_type=F32)
            p3 = jnp.dot(lhs[: 2 * rank], gsplit[j, 2], preferred_element_type=F32)
            low = p1[2 * rank : 3 * rank] + p2[rank : 2 * rank] + p3[:rank]
            ybuf[step, my_chan, j * rank : (j + 1) * rank] = p1[:rank] + (p1[rank : 2 * rank] + p2[:rank] + low)
            push_rows(step, j)

    def gathered(step):
        arrived(ybuf.at[step], n_chan, step)
        return orthonormal(total(ybuf.at[step], n_chan).reshape(tiles, rank, times))

    advance(gathered(0), 1)

    weighted = []
    for j in range(tiles):
        at = slice(j * dpad, (j + 1) * dpad)
        bp = jnp.dot(resp[j], vis_tile(j), preferred_element_type=F32)
        weighted.append(bp * tb)
        for ref, part in ((bsplit, bp), (tsplit, tb)):
            b1, b2, b3 = split3(part)
            ref[0, at] = b1.astype(BF16)
            ref[1, at] = b2.astype(BF16)
            ref[2, at] = b3.astype(BF16)

    arrived(nbuf, n_chan, SUB_ITERS)
    sub = lax.broadcasted_iota(jnp.int32, (GROUP, LANES), 0)
    lane = lax.broadcasted_iota(jnp.int32, (GROUP, LANES), 1)
    eye = jnp.where(sub == lane, F32(1.0), F32(0.0))
    n1, n2, n3 = split3(total(nbuf, n_chan))
    lhs = jnp.concatenate([n1, n2, n3], axis=0).astype(BF16)
    wide = jnp.dot(lhs, spread[...], preferred_element_type=F32)
    wide = wide[:GROUP] + (wide[GROUP : 2 * GROUP] + wide[2 * GROUP :])
    cols = [wide[:, m * LANES : (m + 1) * LANES] for m in range(CL)]
    trace = cols[0][0:1]
    for m in range(1, CL):
        trace = trace + cols[m][m : m + 1]
    recip = F32(1.0) / (F32(RHO_SCALE) * trace / F32(CL))
    inv_rho = [recip[:, j * GROUP : j * GROUP + 1] for j in range(tiles)]
    cols = [jnp.where(sub == m, F32(1.0), F32(0.0)) + cols[m] * recip for m in range(CL)]
    for p in range(CL):
        col = cols[p]
        d = F32(1.0) / col[p : p + 1]
        for m in range(CL):
            if m != p:
                f = cols[m][p : p + 1] * d
                cols[m] = jnp.where(sub == p, f, cols[m] - col * f)
        cols[p] = jnp.where(sub == p, d, -col * d)
    first = jnp.zeros((GROUP, LANES), F32)
    for m in range(CL):
        here = (lax.rem(lane, GROUP) == m) & (lane < tiles * GROUP)
        first = jnp.where(here, jnp.where(sub == m, F32(1.0), F32(0.0)) - cols[m], first)

    def times_of(a, b):
        return jnp.dot(a, b, precision=HIGHEST, preferred_element_type=F32)

    def blocks(m):
        rows = [jnp.where(lax.div(lane, GROUP) == j, m, F32(0.0)) for j in range(tiles)]
        return jnp.concatenate(rows + [jnp.zeros((LANES - tiles * GROUP, LANES), F32)], axis=0)

    advance(gathered(1), 2)

    e1 = blocks(first)
    second = times_of(first, e1)
    e2 = blocks(second)
    third = times_of(second, e1)
    later = times_of(jnp.concatenate([second, third], axis=0), e2)
    powers = [first, second, third, later[:GROUP], later[GROUP:], times_of(later[:GROUP], e2)]
    group = lax.div(lane, GROUP)
    by_tile = []
    for j in range(tiles):
        out = jnp.zeros((GROUP, LANES), F32)
        for p in range(ADMM_ITERS):
            shift = (p - j) * GROUP % LANES
            m = pltpu.roll(powers[p], shift, 1) if shift else powers[p]
            out = jnp.where(group == p, m, out)
        by_tile.append(out)
    packed = by_tile[0]
    for j in range(1, tiles):
        packed = packed + by_tile[j]
    mbuf[my_bl] = packed
    push(mbuf, my_bl, n_bl, along_bl, SUB_ITERS + 1)
    eye_all = jnp.where(lax.rem(lane, GROUP) == sub, F32(1.0), F32(0.0))
    eye_all = jnp.where(lane < tiles * GROUP, eye_all, F32(0.0))
    powers = [eye_all] + powers

    before_ref[...] = lax.dot_general(
        jnp.ones((8, times), F32), jnp.concatenate(weighted, axis=0), NT, precision=HIGHEST, preferred_element_type=F32
    )
    eye_rep = jnp.where((lax.rem(lane, GROUP) == sub) & (group < ADMM_ITERS), F32(1.0), F32(0.0))
    final = powers[ADMM_ITERS - 1] - powers[ADMM_ITERS]
    for j in range(tiles):
        own = jnp.where(group == j, final, F32(0.0))
        both = jnp.concatenate([eye_rep - by_tile[j], own], axis=1) * inv_rho[j]
        q1, q2, q3 = split3(
            lax.dot_general(member_rows, both, TN, precision=HIGHEST, preferred_element_type=F32)
        )
        at = slice(j * dpad, (j + 1) * dpad)
        qsplit[0, at] = q1.astype(BF16)
        qsplit[1, at] = q2.astype(BF16)
        qsplit[2, at] = q3.astype(BF16)

    def stacked(row):
        a, b, c = split3(row)
        at = lax.broadcasted_iota(jnp.int32, (16, row.shape[1]), 0)
        return jnp.where(at == 0, a, jnp.where(at == 1, b, jnp.where(at == 2, c, F32(0.0)))).astype(BF16)

    def row_times(row, parts):
        lhs = stacked(row)
        at = lax.broadcasted_iota(jnp.int32, (16, parts[0].shape[1]), 0)
        acc = jnp.where(at < 1, jnp.dot(lhs, parts[2], preferred_element_type=F32), F32(0.0))
        acc = acc + jnp.where(at < 2, jnp.dot(lhs, parts[1], preferred_element_type=F32), F32(0.0))
        acc = acc + jnp.where(at < 3, jnp.dot(lhs, parts[0], preferred_element_type=F32), F32(0.0))
        return jnp.sum(acc, axis=0, keepdims=True)

    def along_times(lhs, ref):
        acc = lax.dot_general(lhs, ref[2], NT, preferred_element_type=F32)
        acc = acc + lax.dot_general(lhs, ref[1], NT, preferred_element_type=F32)
        return acc + lax.dot_general(lhs, ref[0], NT, preferred_element_type=F32)

    basis = gathered(2).astype(BF16).astype(F32).reshape(tiles * rank, times)
    rows16 = basis.astype(BF16)
    product = along_times(rows16, bsplit) * along_times(rows16, tsplit)
    row_tile = lax.div(lax.broadcasted_iota(jnp.int32, product.shape, 0), rank)
    lane_tile = lax.div(lax.broadcasted_iota(jnp.int32, product.shape, 1), dpad)
    product = jnp.where(row_tile == lane_tile, product, F32(0.0))
    rhs_row = before_ref[0:1] - jnp.sum(product, axis=0, keepdims=True)
    row = row_times(rhs_row, (qsplit[0], qsplit[1], qsplit[2]))
    vbuf[my_id] = row[:, 0:LANES]
    lbuf[my_chan] = row[:, LANES : 2 * LANES]
    push(vbuf, my_id, n_all, everyone, SUB_ITERS + 2)
    push(lbuf, my_chan, n_chan, along_chan, SUB_ITERS + 3)

    part_lane = lax.broadcasted_iota(jnp.int32, (1, 4 * rank), 1)
    for j in range(tiles):
        own = basis[j * rank : (j + 1) * rank]
        wide = jnp.concatenate([own, own, own, jnp.zeros_like(own)], axis=0).astype(BF16)
        v = vis_tile(j)
        proj = lax.dot_general(v, wide, NT, preferred_element_type=F32)
        a, b, c = split3(proj)
        parts = jnp.where(part_lane < rank, a, jnp.where(part_lane < 2 * rank, b, c)).astype(BF16)
        correction = jnp.dot(parts, wide, preferred_element_type=F32)
        clean_ref[:, :, j * tile : (j + 1) * tile, :] = (
            (v.astype(F32) - correction).astype(BF16).reshape(2, chan_dev, tile, times)
        )

    arrived(mbuf, n_bl, SUB_ITERS + 1)
    moments = jnp.where(group < ADMM_ITERS - 1, total(mbuf, n_bl) * F32(1.0 / tiles_all), F32(0.0))
    history = jnp.where(group == 0, eye, pltpu.roll(moments, GROUP, 1))
    gain = jnp.where(group < ADMM_ITERS - 1, history, F32(0.0)) - F32(2.0) * moments
    local = []
    for i in range(1, ADMM_ITERS - 1):
        k = ADMM_ITERS - 2 - i
        local.append(F32(3.0) * powers[k + 1] - powers[k] - F32(2.0) * powers[k + 2])
    local.append(F32(2.0) * (powers[0] - powers[1]))
    apply = [jnp.where(lane == sub + tiles * GROUP, F32(1.0), F32(0.0))]
    for k in range(ADMM_ITERS - 2, -1, -1):
        pad = jnp.zeros((LANES - len(apply) * GROUP, LANES), F32)
        apply.insert(0, local[k] + times_of(gain, jnp.concatenate(apply + [pad], axis=0)))
    factor = F32((channels * tile * times) ** 0.5)
    pad = jnp.zeros((LANES - len(apply) * GROUP, LANES), F32)
    apply = jnp.concatenate(apply + [pad], axis=0) * F32((channels * tile * times) ** 0.5 / tiles_all)
    parts = tuple(part.astype(BF16) for part in split3(apply))
    arrived(vbuf, n_all, SUB_ITERS + 2)
    arrived(lbuf, n_chan, SUB_ITERS + 3)
    x = row_times(tree(vbuf, n_all), parts) + total(lbuf, n_chan) * factor
    x = jnp.broadcast_to(x, (8, LANES))
    for j in range(tiles):
        at = x if j == 0 else pltpu.roll(x, LANES - j * GROUP, 1)
        gains_ref[j : j + 1, :] = at[0:1, 0:CL]
    cons_ref[...] = pltpu.roll(x, LANES - tiles * GROUP, 1)[0:1, 0:CL]

    for step in range(SUB_ITERS):
        sent(ybuf.at[step], n_chan, step)
    sent(nbuf, n_chan, SUB_ITERS)
    sent(mbuf, n_bl, SUB_ITERS + 1)
    sent(vbuf, n_all, SUB_ITERS + 2)
    sent(lbuf, n_chan, SUB_ITERS + 3)


def store_kernel(clean_in, gains_in, cons_in, clean_out, gains_out, cons_out, sems):
    parts, chans = clean_in.shape[:2]
    stores = [
        pltpu.make_async_copy(gains_in, gains_out, sems.at[0]),
        pltpu.make_async_copy(cons_in, cons_out, sems.at[1]),
    ]
    for p in range(parts):
        for c in range(chans):
            stores.append(
                pltpu.make_async_copy(clean_in.at[p, c], clean_out.at[p, c], sems.at[2 + p * chans + c])
            )
    for store in stores:
        store.start()
    for store in stores:
        store.wait()


def per_device(vis, station_pair_index, station_coords, dir_lm, time_beam, dir_cluster, seed_block):
    n_chan = lax.axis_size("chan")
    n_bl = lax.axis_size("bl")
    chan_dev, base_dev, times = vis.shape[1:]
    tiles, _, rank = seed_block.shape
    tile = base_dev // tiles
    dirs = dir_lm.shape[0]
    dpad = (dirs + 15) // 16 * 16
    stations = station_coords.shape[0]
    vmem = pl.BlockSpec(memory_space=pltpu.VMEM)
    anywhere = pl.BlockSpec(memory_space=pl.ANY)
    shapes = (
        jax.ShapeDtypeStruct(vis.shape, BF16),
        jax.ShapeDtypeStruct((tiles, CL), F32),
        jax.ShapeDtypeStruct((1, CL), F32),
    )
    results = pl.pallas_call(
        functools.partial(main_kernel, n_chan, n_bl, chan_dev * n_chan),
        out_shape=tuple(pltpu.VMEM(s.shape, s.dtype) for s in shapes),
        in_specs=[anywhere] * 7,
        out_specs=(vmem, vmem, vmem),
        scratch_shapes=[
            pltpu.VMEM(vis.shape, BF16),
            pltpu.VMEM((2, base_dev), jnp.int32),
            pltpu.VMEM((2, stations), F32),
            pltpu.VMEM((2, dirs), F32),
            pltpu.VMEM((dirs, times), F32),
            pltpu.VMEM((1, dirs), jnp.int32),
            pltpu.VMEM((tiles, rank, times), jnp.int32),
            pltpu.VMEM((tiles, 3, times, times), BF16),
            pltpu.VMEM((tiles, dpad, 2 * chan_dev * tile), BF16),
            pltpu.VMEM((8, LANES), F32),
            pltpu.VMEM((dpad, times), F32),
            pltpu.VMEM((8, LANES), jnp.int32),
            pltpu.VMEM((GROUP, stations), F32),
            pltpu.VMEM((GROUP, base_dev), F32),
            pltpu.VMEM((3, tiles * dpad, times), BF16),
            pltpu.VMEM((3, tiles * dpad, times), BF16),
            pltpu.VMEM((3, tiles * dpad, 2 * LANES), BF16),
            pltpu.VMEM((8, tiles * dpad), F32),
            pltpu.VMEM((tiles * dpad, CL * LANES), BF16),
            pltpu.VMEM((SUB_ITERS, n_chan, tiles * rank, times), F32),
            pltpu.VMEM((n_chan, GROUP, tiles * dpad), F32),
            pltpu.VMEM((n_bl, GROUP, LANES), F32),
            pltpu.VMEM((n_chan * n_bl, 1, LANES), F32),
            pltpu.VMEM((n_chan, 1, LANES), F32),
            pltpu.SemaphoreType.DMA((SUB_ITERS + 4,)),
            pltpu.SemaphoreType.DMA((SUB_ITERS + 4,)),
            pltpu.SemaphoreType.DMA((tiles,)),
            pltpu.SemaphoreType.DMA((6,)),
        ],
        compiler_params=pltpu.CompilerParams(
            collective_id=0, has_side_effects=True, vmem_limit_bytes=32 * 1024 * 1024
        ),
    )(
        *(
            pltpu.with_memory_space_constraint(a, pltpu.HBM)
            for a in (
                vis,
                station_pair_index.T,
                station_coords.T,
                dir_lm.T,
                time_beam,
                dir_cluster.reshape(1, dirs),
                jnp.swapaxes(seed_block, 1, 2),
            )
        )
    )
    clean, gains, consensus = pl.pallas_call(
        store_kernel,
        out_shape=shapes,
        in_specs=[vmem] * 3,
        out_specs=(anywhere, anywhere, anywhere),
        scratch_shapes=[pltpu.SemaphoreType.DMA((2 + 2 * chan_dev,))],
        compiler_params=pltpu.CompilerParams(vmem_limit_bytes=8 * 1024 * 1024),
    )(*results)
    return clean, gains, consensus.reshape(CL)


def solution(mesh):
    placed = (P(None, "chan", "bl", None), P("bl", None), P(), P(), P(), P(), P("bl", None, None))
    return jax.shard_map(
        per_device,
        mesh=mesh,
        in_specs=placed,
        out_specs=(P(None, "chan", "bl", None), P("bl", None), P()),
        check_vma=False,
    )
```
